512 devices in a mesh: section: 4 (over x), dom: 128 (over y, z, core).
Axes of the slice: x: 4, y: 8, z: 8, core: 2. Of those that a mesh axis runs over, the one named last changes fastest.
Arguments:
- features: bfloat16 [2, 131072, 128], P(None, 'dom'), may hold values from -6 to 6
- counts: int32 [128], P('dom'), may hold values from 512 to 1024, as said below
- row_blocks: int32 [3072], P('dom'), may hold values from 0 to 7
- col_blocks: int32 [3072], P('dom'), may hold values from 0 to 9, as said below
- adjacency: bfloat16 [3072, 128, 128], P('dom'), may hold values from -0.3125 to 0.3125
- send_up: int32 [128], P('dom'), may hold values from 0 to 3
- send_down: int32 [128], P('dom'), may hold values from 0 to 3
- w_message: bfloat16 [8, 128, 128], P('section'), may hold values from -0.5 to 0.5
- w_hidden: bfloat16 [8, 256, 128], P('section'), may hold values from -0.375 to 0.375
- b_hidden: bfloat16 [8, 128], P('section'), may hold values from -3 to 3
- w_out: bfloat16 [8, 128, 128], P('section'), may hold values from -0.5 to 0.5
- b_out: bfloat16 [8, 128], P('section'), may hold values from -3 to 3
- gain: bfloat16 [8, 128], P('section'), may hold values from 0.099609375 to 1.8984375
Outputs:
- checkpoints: bfloat16 [4, 2, 131072, 128], P('section', None, 'dom')
The draws below stay inside these ranges and needn't reach their ends.
Inputs may be any that keep to these rules, and one draw needn't show every extreme that they name: `counts`: some partition has exactly 1024 live nodes. `col_blocks`: each of the last 2 extended block indices is named by some adjacency block of every partition.
All inputs are finite; a program needn't handle non-finite values.
Results may differ from the reference program's by a relative error of at most 0.015.
Values may be sent and summed in bfloat16 or wider, within the bound.
No kernel may reach another device: no remote copies, remote signals or barrier semaphores. Data moves between devices by JAX's collectives and lax.ppermute only.
A program may use at most 64 MiB of HBM per device.

```python
import jax
import jax.numpy as jnp
from jax import lax

D = 128
BLOCK = 128
NB = 8
LS = 2
MB = 2
HB = 1
NBLK = 24
NODES_DEV = 1024
NODES = 131072
LAYERS = 8
N_SECTION = 4
N_DOM = 128


def draw_counts(key, part):
    first_key, second_key = jax.random.split(jax.random.fold_in(key, 11))
    values = jax.random.randint(first_key, (N_DOM,), NODES_DEV // 2, NODES_DEV + 1)
    chosen = jax.random.randint(second_key, (), 0, N_DOM)
    return jnp.where(jnp.arange(N_DOM) == chosen, NODES_DEV, values).astype(jnp.int32)


def draw_col_blocks(key, part):
    device_keys = jax.random.split(jax.random.fold_in(key, 23), N_DOM)

    def one_device(device_key):
        first_key, second_key = jax.random.split(device_key)
        columns = jax.random.randint(first_key, (NBLK,), 0, NB + 2 * HB)
        order = jax.random.permutation(second_key, NBLK)
        slots = NB + jnp.arange(2 * HB)
        return columns.at[order[:2 * HB]].set(slots)
    return jax.vmap(one_device)(device_keys).reshape(-1).astype(jnp.int32)


def place_ends(entries, stream_key, smallest, largest):
    longest = entries.shape.index(max(entries.shape))
    spots = []
    for shift in (0, 1):
        where = [jax.random.randint(jax.random.fold_in(stream_key, axis), (), 0, length) for axis, length in enumerate(entries.shape)]
        where[longest] = (where[longest] + shift) % entries.shape[longest]
        spots.append(tuple(where))
    return entries.at[spots[0]].set(smallest).at[spots[1]].set(largest)


def levels(own_key, shape, pieces, smallest, largest):
    def one(dim, parts):
        steps = jax.random.uniform(jax.random.fold_in(jax.random.fold_in(own_key, 6), dim), (parts,), jnp.float32, smallest / len(pieces), largest / len(pieces))
        return jnp.repeat(jnp.exp(steps), shape[dim] // parts).reshape((-1,) + (1,) * (len(shape) - dim - 1))

    loudness = one(*pieces[0])
    for cut in pieces[1:]:
        loudness = loudness * one(*cut)
    return loudness


def noise(own_key, shape, deviation, most, pieces=(), kind=jnp.bfloat16):
    drawn = jax.random.normal(own_key, shape, jnp.float32) * deviation
    if len(pieces) > 0:
        drawn = levels(own_key, shape, pieces, -0.22, 0.18) * drawn
    return jnp.clip(drawn, min=-most, max=most).astype(kind)


def setup_inputs(seed: int = 0) -> dict:
    splits = jax.random.split(jax.random.key(seed), 14)
    return {
        "features": noise(splits[0], (MB, NODES, D), 1.0, 6.0, ((1, 128),)),
        "counts": draw_counts(jax.random.fold_in(splits[13], 71), 0),
        "row_blocks": place_ends(jax.random.randint(splits[2], (N_DOM * NBLK,), 0, NB), jax.random.fold_in(splits[2], 1), 0, NB - 1).astype(jnp.int32),
        "col_blocks": draw_col_blocks(jax.random.fold_in(splits[13], 71), 0),
        "adjacency": noise(splits[4], (N_DOM * NBLK, BLOCK, BLOCK), (3 * BLOCK) ** -0.5, 0.3125, ((0, 128),)),
        "send_up": place_ends(jax.random.randint(splits[5], (N_DOM * HB,), 0, NB // 2), jax.random.fold_in(splits[5], 1), 0, (NB // 2) - 1).astype(jnp.int32),
        "send_down": place_ends(jax.random.randint(splits[6], (N_DOM * HB,), 0, NB // 2), jax.random.fold_in(splits[6], 1), 0, (NB // 2) - 1).astype(jnp.int32),
        "w_message": noise(splits[7], (LAYERS, D, D), D ** -0.5, 0.5, ((0, 4),)),
        "w_hidden": noise(splits[8], (LAYERS, 2 * D, D), (2 * D) ** -0.5, 0.375, ((0, 4),)),
        "b_hidden": noise(splits[9], (LAYERS, D), 0.5, 3.0, ((0, 4),)),
        "w_out": noise(splits[10], (LAYERS, D, D), D ** -0.5, 0.5, ((0, 4),)),
        "b_out": noise(splits[11], (LAYERS, D), 0.5, 3.0, ((0, 4),)),
        "gain": jnp.clip(1.0 + 0.18 * jax.random.normal(splits[12], (LAYERS, D), jnp.float32), 0.099609375, 1.8984375).astype(jnp.bfloat16),
    }


def process_layer(node_state, live_rows, graph_data, layer_index, weights):
    row_list, col_list, adj_blocks, up_list, down_list = graph_data
    w_message, w_hidden, b_hidden, w_out, b_out, gain = weights
    messages = jax.nn.silu(jnp.dot(node_state, w_message[layer_index], preferred_element_type=jnp.float32)).astype(jnp.bfloat16)
    blocks = messages.reshape(N_DOM, NB, BLOCK, D)
    partition = jnp.arange(N_DOM, dtype=jnp.int32)[:, None]
    sent_up = blocks[partition, up_list]
    sent_down = blocks[partition, down_list]
    empty_blocks = jnp.zeros((1, HB, BLOCK, D), jnp.bfloat16)
    below = jnp.concatenate([empty_blocks, sent_up[:-1]], axis=0)
    above = jnp.concatenate([sent_down[1:], empty_blocks], axis=0)
    extended = jnp.concatenate([blocks, below, above], axis=1)

    def per_device(device_item):
        adj_dev, rows_dev, cols_dev, ext_dev = device_item
        picked = ext_dev[cols_dev]
        products = jnp.einsum('bij,bjd->bid', adj_dev.astype(jnp.float32), picked.astype(jnp.float32))
        return jax.ops.segment_sum(products, rows_dev, num_segments=NB)
    summed = lax.map(per_device, (adj_blocks, row_list, col_list, extended))
    agg = summed.reshape(-1, D).astype(jnp.bfloat16)
    joined = jnp.concatenate([node_state, agg], axis=1)
    hidden = jax.nn.silu(jnp.dot(joined, w_hidden[layer_index], preferred_element_type=jnp.float32) + b_hidden[layer_index].astype(jnp.float32)).astype(jnp.bfloat16)
    update = jnp.dot(hidden, w_out[layer_index], preferred_element_type=jnp.float32) + b_out[layer_index].astype(jnp.float32)
    average = lax.optimization_barrier(jnp.mean(update, axis=-1, keepdims=True))
    spread = lax.optimization_barrier(jnp.mean((update - average) ** 2, axis=-1, keepdims=True))
    normed = (update - average) * lax.rsqrt(spread + 1e-05) * gain[layer_index].astype(jnp.float32)
    return (live_rows * (node_state.astype(jnp.float32) + normed)).astype(jnp.bfloat16)

def reference(features, counts, row_blocks, col_blocks, adjacency, send_up, send_down, w_message, w_hidden, b_hidden, w_out, b_out, gain):
    node_total = features.shape[1]
    node_index = jnp.arange(node_total, dtype=jnp.int32)
    owner_part = node_index // NODES_DEV
    live_rows = (node_index % NODES_DEV < counts[owner_part]).astype(jnp.float32)[:, None]
    graph_data = (row_blocks.reshape(N_DOM, NBLK), col_blocks.reshape(N_DOM, NBLK), adjacency.reshape(N_DOM, NBLK, BLOCK, BLOCK), send_up.reshape(N_DOM, HB), send_down.reshape(N_DOM, HB))
    weights = (w_message, w_hidden, b_hidden, w_out, b_out, gain)
    per_section = [[None] * MB for section_index in range(N_SECTION)]
    for batch_index in range(MB):
        node_state = (live_rows * features[batch_index].astype(jnp.float32)).astype(jnp.bfloat16)
        for layer_index in range(LAYERS):
            node_state = process_layer(node_state, live_rows, graph_data, layer_index, weights)
            if (layer_index + 1) % LS == 0:
                per_section[layer_index // LS][batch_index] = node_state
    return jnp.stack([jnp.stack(section_list) for section_list in per_section])
```

```python
import jax
import jax.numpy as jnp
from jax import lax
from jax.experimental import pallas as pl
from jax.experimental.pallas import tpu as pltpu
from jax.sharding import PartitionSpec as P

BF = jnp.bfloat16
F32 = jnp.float32
VM = pl.BlockSpec(memory_space=pltpu.VMEM)
SM = pl.BlockSpec(memory_space=pltpu.SMEM)


def call(body, outs, ins, name, scratch=(), room=8):
    return pl.pallas_call(
        body,
        out_shape=outs,
        in_specs=ins,
        out_specs=jax.tree.map(lambda _: VM, outs),
        scratch_shapes=list(scratch),
        name=name,
        compiler_params=pltpu.CompilerParams(vmem_limit_bytes=room << 20),
    )


def silu(v):
    return 0.5 * v * (1.0 + jnp.tanh(0.5 * v))


def twice(w):
    zero = jnp.zeros_like(w)
    return jnp.concatenate(
        [jnp.concatenate([w, zero], axis=1), jnp.concatenate([zero, w], axis=1)], axis=0
    )


def pack_body(wm, wh, bh, wo, bo, gain, out):
    d = wm.shape[1]
    for i in range(2):
        out[i * d : (i + 1) * d] = wm[i]
        out[2 * d + i * 2 * d : 2 * d + (i + 1) * 2 * d] = wh[i]
        w = wo[i].astype(F32)
        out[6 * d + i * d : 6 * d + (i + 1) * d] = (w - jnp.mean(w, axis=1, keepdims=True)).astype(BF)
    b = bo[...].astype(F32)
    b = b - jnp.mean(b, axis=1, keepdims=True)
    high = b.astype(BF)
    low = (b - high.astype(F32)).astype(BF)
    pad = jnp.zeros((8, d), F32)
    vectors = [bh[...].astype(F32), high.astype(F32), low.astype(F32), gain[...].astype(F32), pad]
    out[8 * d :] = jnp.concatenate(vectors, axis=0).astype(BF)


def prep_body(meta, rows, cols, x, adj, h, send, dense, acc):
    count, even = meta[0], meta[1]
    n, d = x.shape[1], x.shape[2]
    blk = adj.shape[1]
    live = lax.broadcasted_iota(jnp.int32, (n, d), 0) < count
    for m in range(2):
        h[:, m * d : (m + 1) * d] = jnp.where(live, x[m], jnp.zeros_like(x[m]))
    for i in range(2):
        send[i] = h[pl.ds(pl.multiple_of(meta[2 + i] * blk, blk), blk), :]
    acc[...] = jnp.zeros_like(acc)
    last = n // blk
    for k in range(adj.shape[0]):
        c = cols[k]
        c = jnp.where(c < last, c, jnp.where(even == 1, 2 * last + 1 - c, c))
        at = (rows[k], c)
        acc[at] = acc[at] + adj[k].astype(F32)
    for r in range(n // blk):
        for c in range(last + 2):
            dense[r * blk : (r + 1) * blk, c * blk : (c + 1) * blk] = acc[r, c].astype(BF)


def messages(h, pack, i):
    d = pack.shape[1]
    wm = twice(pack[i * d : (i + 1) * d])
    return silu(jnp.dot(h, wm, preferred_element_type=F32)).astype(BF)


def update(h, a_local, a_halo, m, halo, live, pack, i):
    d = pack.shape[1]
    agg = jnp.dot(a_local, m, preferred_element_type=F32)
    agg = (agg + jnp.dot(a_halo, halo, preferred_element_type=F32)).astype(BF)
    wh = pack[2 * d + i * 2 * d : 2 * d + (i + 1) * 2 * d]
    wo = twice(pack[6 * d + i * d : 6 * d + (i + 1) * d])
    v = pack[8 * d :].astype(F32)

    def row(j):
        r = v[j + i : j + i + 1]
        return jnp.concatenate([r, r], axis=1)

    pre = jnp.concatenate(
        [
            jnp.dot(
                jnp.concatenate([h[:, s : s + d], agg[:, s : s + d]], axis=1),
                wh,
                preferred_element_type=F32,
            )
            for s in (0, d)
        ],
        axis=1,
    )
    hidden = silu(pre + row(0)).astype(BF)
    c = jnp.dot(hidden, wo, preferred_element_type=F32) + (row(2) + row(4))
    mean = twice(jnp.full((d, d), 1.0 / d, BF))
    var = jnp.dot((c * c).astype(BF), mean, preferred_element_type=F32)
    new = h.astype(F32) + c * lax.rsqrt(var + 1e-05) * row(6)
    return jnp.where(live, new, 0.0).astype(BF)


def first_body(meta, h, haloq, halor, pack, m, halo):
    m[...] = messages(h[...], pack, 0)
    blk = halor.shape[0]
    halo[:blk] = messages(haloq[meta[1]], pack, 0)
    halo[blk:] = messages(halor[...], pack, 0)


def gather_halo(meta, haloq, halor):
    return jnp.concatenate([haloq[meta[1]], halor[...]], axis=0)


def send_body(step, first):
    def body(meta, h, m, haloq, halor, dense, pack, nxt, outq, outr):
        n = m.shape[0]
        blk = halor.shape[0] // (2 if first else 1)
        halo = halor[...] if first else gather_halo(meta, haloq, halor)
        for i, out in ((0, outq), (1, outr)):
            at = pl.ds(pl.multiple_of(meta[2 + i] * blk, blk), blk)
            row = meta[2 + i] * blk + lax.broadcasted_iota(jnp.int32, (blk, h.shape[1]), 0)
            new = update(
                h[at, :], dense[at, :n], dense[at, n:], m[...], halo, row < meta[0], pack, step % 2
            )
            out[...] = messages(new, nxt, (step + 1) % 2)

    return body


def rows_body(step, first, last):
    def body(meta, h, m, haloq, halor, dense, pack, nxt, *outs):
        n, d2 = m.shape
        halo = halor[...] if first else gather_halo(meta, haloq, halor)
        chunk = 256
        for r in range(0, n, chunk):
            at = slice(r, r + chunk)
            live = r + lax.broadcasted_iota(jnp.int32, (chunk, d2), 0) < meta[0]
            new = update(h[at], dense[at, :n], dense[at, n:], m[...], halo, live, pack, step % 2)
            if last:
                outs[0][0, at] = new[:, : d2 // 2]
                outs[0][1, at] = new[:, d2 // 2 :]
            else:
                outs[0][at] = new
                outs[1][at] = messages(new, nxt, (step + 1) % 2)

    return body


def shards(
    features,
    counts,
    row_blocks,
    col_blocks,
    adjacency,
    send_up,
    send_down,
    w_message,
    w_hidden,
    b_hidden,
    w_out,
    b_out,
    gain,
):
    n, d = features.shape[1:]
    blk = adjacency.shape[1]
    doms = lax.axis_size("dom")
    sections = lax.axis_size("section")
    layers = w_message.shape[0]
    odd = lax.axis_index("dom") % 2
    even = 1 - odd
    near = jnp.where(odd == 1, send_down[0], send_up[0])
    far = jnp.where(odd == 1, send_up[0], send_down[0])
    meta = jnp.stack([counts[0], even, near, far]).astype(jnp.int32)
    pairs = [[i, i + 1] for i in range(0, doms, 2)]
    across = [(i, i + 1) for i in range(1, doms - 1, 2)] + [(i + 1, i) for i in range(1, doms - 1, 2)]

    def s(*shape, dtype=BF):
        return jax.ShapeDtypeStruct(shape, dtype)

    def exchange(q, r):
        halor = lax.ppermute(r, "dom", across)
        haloq = lax.all_gather(q, "dom", axis_index_groups=pairs)
        return haloq, halor

    rows = w_message.shape[0] * 4 * d + 16
    own = call(pack_body, s(rows, d), [VM] * 6, "pack")(
        w_message, w_hidden, b_hidden, w_out, b_out, gain
    )
    packs = [
        lax.ppermute(own, "section", [(i, i + k) for i in range(sections - k)])
        for k in range(sections - 1, 0, -1)
    ] + [own]
    h, send, dense = call(
        prep_body,
        (s(n, 2 * d), s(2, blk, 2 * d), s(n, n + 2 * blk)),
        [SM, SM, SM, VM, VM],
        "prep",
        [pltpu.VMEM((n // blk, n // blk + 2, blk, blk), F32)],
        16,
    )(meta, row_blocks, col_blocks, features, adjacency)
    haloq, halor = exchange(send[0], send[1])
    m, halor = call(first_body, (s(n, 2 * d), s(2 * blk, 2 * d)), [SM] + [VM] * 4, "first")(
        meta, h, haloq, halor, packs[0]
    )
    steps = layers * sections
    for step in range(steps):
        pack = packs[step // layers]
        nxt = packs[min(step + 1, steps - 1) // layers]
        args = (meta, h, m, haloq, halor, dense, pack, nxt)
        ins = [SM] + [VM] * 7
        if step + 1 == steps:
            out = call(rows_body(step, step == 0, True), s(2, n, d), ins, f"rows{step}")(*args)
            return out[None]
        q, r = call(
            send_body(step, step == 0), (s(blk, 2 * d), s(blk, 2 * d)), ins, f"send{step}"
        )(*args)
        haloq, halor = exchange(q, r)
        h, m = call(
            rows_body(step, step == 0, False), (s(n, 2 * d), s(n, 2 * d)), ins, f"rows{step}"
        )(*args)


def solution(mesh):
    placed = (
        P(None, "dom", None),
        P("dom"),
        P("dom"),
        P("dom"),
        P("dom", None, None),
        P("dom"),
        P("dom"),
        P("section", None, None),
        P("section", None, None),
        P("section", None),
        P("section", None, None),
        P("section", None),
        P("section", None),
    )
    return jax.shard_map(
        shards,
        mesh=mesh,
        in_specs=placed,
        out_specs=P("section", None, "dom", None),
        check_vma=False,
    )
```

```python
import jax
import jax.numpy as jnp
from jax import lax
from jax.experimental import pallas as pl
from jax.experimental.pallas import tpu as pltpu
from jax.sharding import PartitionSpec as P


BF = jnp.bfloat16
F32 = jnp.float32
VM = pl.BlockSpec(memory_space=pltpu.VMEM)
SM = pl.BlockSpec(memory_space=pltpu.SMEM)
HB = pl.BlockSpec(memory_space=pltpu.HBM)
CHUNK = 256


def call(body, outs, ins, scratch=(), room=8, spaces=None):
    return pl.pallas_call(
        body,
        out_shape=outs,
        in_specs=ins,
        out_specs=spaces or jax.tree.map(lambda _: VM, outs),
        scratch_shapes=list(scratch),
        compiler_params=pltpu.CompilerParams(vmem_limit_bytes=room << 20),
    )


def in_hbm(a):
    return pltpu.with_memory_space_constraint(a, pltpu.HBM)


def dot(a, b):
    return jnp.dot(a, b, preferred_element_type=F32)


def silu_of_twice(u):
    return (u + u * jnp.tanh(u)).astype(BF)


def twice(w):
    zero = jnp.zeros_like(w)
    return jnp.concatenate(
        [jnp.concatenate([w, zero], axis=1), jnp.concatenate([zero, w], axis=1)], axis=0
    )


def begin_body(meta, x, wm, wh, bh, wo, bo, gain, out, sq, sr, xs, am, ah, ao, vb, vo, vg, sem):
    d = wm.shape[2]
    blk = sq.shape[0]
    copies = [
        pltpu.make_async_copy(src, dst, sem.at[i])
        for i, (src, dst) in enumerate(
            [(wm, am), (wh, ah), (wo, ao), (bh, vb), (bo, vo), (gain, vg)]
            + [
                (x.at[:, pl.ds(pl.multiple_of(meta[2 + i] * blk, blk), blk), :], xs.at[i])
                for i in range(2)
            ]
        )
    ]
    for copy in copies:
        copy.start()
    for copy in copies[:6]:
        copy.wait()
    for i in range(2):
        out[i * d : (i + 1) * d] = (am[i].astype(F32) * 0.5).astype(BF)
        at = 2 * d + i * 2 * d
        out[at : at + 2 * d] = (ah[i].astype(F32) * 0.5).astype(BF)
        w = ao[i].astype(F32)
        at = 6 * d + i * d
        out[at : at + d] = (w - jnp.mean(w, axis=1, keepdims=True)).astype(BF)
    b = vo[...].astype(F32)
    b = b - jnp.mean(b, axis=1, keepdims=True)
    high = b.astype(BF).astype(F32)
    pad = jnp.zeros((8, d), F32)
    vectors = [vb[...].astype(F32) * 0.5, high, b - high, vg[...].astype(F32), pad]
    out[8 * d :] = jnp.concatenate(vectors, axis=0).astype(BF)
    for copy in copies[6:]:
        copy.wait()
    for i, dst in ((0, sq), (1, sr)):
        row = meta[2 + i] * blk + lax.broadcasted_iota(jnp.int32, (blk, d), 0)
        for m in range(2):
            dst[:, m * d : (m + 1) * d] = jnp.where(row < meta[0], xs[i, m], jnp.zeros_like(xs[i, m]))


def prep_body(meta, rows, cols, x, adj, h, hs, dense, ds, mask, ms, pick, acc, xv, av, sem):
    count, even = meta[0], meta[1]
    n, d = xv.shape[1], xv.shape[2]
    blk = av.shape[1]
    copies = [
        pltpu.make_async_copy(x, xv, sem.at[0]),
        pltpu.make_async_copy(adj, av, sem.at[1]),
    ]
    for copy in copies:
        copy.start()
    acc[...] = jnp.zeros_like(acc)
    mask[...] = jnp.where(
        lax.broadcasted_iota(jnp.int32, (n, 2 * d), 0) < count, jnp.float32(1), jnp.float32(0)
    ).astype(BF)
    for i in range(2):
        chosen = jnp.where(even == i, jnp.float32(1), jnp.float32(0))
        pick[i] = jnp.full((blk, 2 * d), chosen, F32).astype(BF)
    copies[0].wait()
    for m in range(2):
        h[:, m * d : (m + 1) * d] = xv[m] * mask[:, :d]
    copies[1].wait()
    last = n // blk
    for k in range(av.shape[0]):
        c = cols[k]
        c = jnp.where(c < last, c, jnp.where(even == 1, 2 * last + 1 - c, c))
        at = (rows[k], c)
        acc[at] = acc[at] + av[k].astype(F32)
    for r in range(n // blk):
        for c in range(last + 2):
            dense[r * blk : (r + 1) * blk, c * blk : (c + 1) * blk] = acc[r, c].astype(BF)
    for i in range(2):
        at = pl.ds(pl.multiple_of(meta[2 + i] * blk, blk), blk)
        to = slice(i * blk, (i + 1) * blk)
        hs[to] = h[at, :]
        ms[to] = mask[at, :]
        ds[to] = dense[at, :]


def message_weight(pack, i):
    d = pack.shape[1]
    return twice(pack[i * d : (i + 1) * d])


def gather_halo(pick, haloq, halor):
    near = haloq[0] * pick[0] + haloq[1] * pick[1]
    return jnp.concatenate([near, halor[...]], axis=0)


def first_body(h, pick, haloq, halor, pack, m, halo):
    w = message_weight(pack, 0)
    m[...] = silu_of_twice(dot(h[...], w))
    halo[...] = silu_of_twice(dot(gather_halo(pick, haloq, halor), w))


def layer(h, m, halo, dense, mask, pack, i, agg, hidden, c, chunk):
    d = pack.shape[1]
    n = m.shape[0]
    rows = [slice(r, r + chunk) for r in range(0, h.shape[0], chunk)]
    wh = pack[2 * d + i * 2 * d : 2 * d + (i + 1) * 2 * d]
    wo = twice(pack[6 * d + i * d : 6 * d + (i + 1) * d])
    v = pack[8 * d :].astype(F32)

    def row(j):
        r = v[j + i : j + i + 1]
        return jnp.concatenate([r, r], axis=1)

    for at in rows:
        agg[at] = (dot(dense[at, :n], m[...]) + dot(dense[at, n:], halo)).astype(BF)
    b = row(0)
    for at in rows:
        pre = [
            dot(jnp.concatenate([h[at, s : s + d], agg[at, s : s + d]], axis=1), wh) for s in (0, d)
        ]
        hidden[at] = silu_of_twice(jnp.concatenate(pre, axis=1) + b)
    b = row(2) + row(4)
    for at in rows:
        c[at] = dot(hidden[at], wo) + b
    mean = twice(jnp.full((d, d), 1.0 / d, BF))
    gain = row(6)
    for at in rows:
        now = c[at]
        var = dot((now * now).astype(BF), mean)
        new = (h[at].astype(F32) + now * lax.rsqrt(var + 1e-05) * gain).astype(BF) * mask[at]
        yield at, new


def send_body(step, first):
    def body(hs, m, pick, haloq, halor, ds, ms, pack, nxt, new_hs, outq, outr, agg, hidden, c):
        blk = outq.shape[0]
        halo = halor[...] if first else gather_halo(pick, haloq, halor)
        for at, new in layer(hs, m, halo, ds, ms, pack, step % 2, agg, hidden, c, 2 * blk):
            new_hs[at] = new
            out = silu_of_twice(dot(new, message_weight(nxt, (step + 1) % 2)))
            outq[...] = out[:blk]
            outr[...] = out[blk:]

    return body


def rows_body(step, first):
    def body(h, m, pick, haloq, halor, dense, mask, pack, nxt, new_h, new_m, agg, hidden, c):
        halo = halor[...] if first else gather_halo(pick, haloq, halor)
        for at, new in layer(h, m, halo, dense, mask, pack, step % 2, agg, hidden, c, CHUNK):
            new_h[at] = new
        w = message_weight(nxt, (step + 1) % 2)
        for r in range(0, h.shape[0], CHUNK):
            at = slice(r, r + CHUNK)
            new_m[at] = silu_of_twice(dot(new_h[at], w))

    return body


def last_body(step):
    def body(h, m, pick, haloq, halor, dense, mask, pack, out, agg, hidden, c, stage, sem):
        halo = gather_halo(pick, haloq, halor)
        d = pack.shape[1]
        copies = []
        for at, new in layer(h, m, halo, dense, mask, pack, step % 2, agg, hidden, c, CHUNK):
            stage[0, at] = new[:, :d]
            stage[1, at] = new[:, d:]
            copies.append(
                pltpu.make_async_copy(stage.at[:, at, :], out.at[:, at, :], sem.at[len(copies)])
            )
            copies[-1].start()
        for copy in copies:
            copy.wait()

    return body


def shards(
    features,
    counts,
    row_blocks,
    col_blocks,
    adjacency,
    send_up,
    send_down,
    w_message,
    w_hidden,
    b_hidden,
    w_out,
    b_out,
    gain,
):
    n, d = features.shape[1:]
    blk = adjacency.shape[1]
    doms = lax.axis_size("dom")
    sections = lax.axis_size("section")
    layers = w_message.shape[0]
    odd = lax.axis_index("dom") % 2
    near = jnp.where(odd == 1, send_down[0], send_up[0])
    far = jnp.where(odd == 1, send_up[0], send_down[0])
    meta = jnp.stack([counts[0], 1 - odd, near, far]).astype(jnp.int32)
    pairs = [[i, i + 1] for i in range(0, doms, 2)]
    across = [(i, i + 1) for i in range(1, doms - 1, 2)] + [(i + 1, i) for i in range(1, doms - 1, 2)]

    def s(*shape, dtype=BF):
        return jax.ShapeDtypeStruct(shape, dtype)

    def exchange(q, r):
        halor = lax.ppermute(r, "dom", across)
        haloq = lax.all_gather(q, "dom", axis_index_groups=pairs)
        return haloq, halor

    def fetch(own, k):
        return lax.ppermute(own, "section", [(i, i + k) for i in range(sections - k)])

    vec = pltpu.VMEM((layers, d), BF)
    own, q, r = call(
        begin_body,
        (s(layers * 4 * d + 16, d), s(blk, 2 * d), s(blk, 2 * d)),
        [SM] + [HB] * 7,
        [
            pltpu.VMEM((2, 2, blk, d), BF),
            pltpu.VMEM((layers, d, d), BF),
            pltpu.VMEM((layers, 2 * d, d), BF),
            pltpu.VMEM((layers, d, d), BF),
            vec,
            vec,
            vec,
            pltpu.SemaphoreType.DMA((8,)),
        ],
    )(meta, *map(in_hbm, (features, w_message, w_hidden, b_hidden, w_out, b_out, gain)))
    packs = [fetch(own, sections - 1)]
    wide = n + 2 * blk
    halor = lax.ppermute(r, "dom", across)
    prep = call(
        prep_body,
        (
            s(n, 2 * d),
            s(2 * blk, 2 * d),
            s(n, wide),
            s(2 * blk, wide),
            s(n, 2 * d),
            s(2 * blk, 2 * d),
            s(2, blk, 2 * d),
        ),
        [SM, SM, SM, HB, HB],
        [
            pltpu.VMEM((n // blk, n // blk + 2, blk, blk), F32),
            pltpu.VMEM(features.shape, BF),
            pltpu.VMEM(adjacency.shape, BF),
            pltpu.SemaphoreType.DMA((2,)),
        ],
        16,
    )
    h, hs, dense, ds, mask, ms, pick = prep(meta, row_blocks, col_blocks, in_hbm(features), in_hbm(adjacency))
    q, pick = lax.optimization_barrier((q, pick))
    haloq = lax.all_gather(q, "dom", axis_index_groups=pairs)
    later, haloq = lax.optimization_barrier((own, haloq))
    packs += [fetch(later, k) for k in range(sections - 2, 0, -1)] + [own]
    m, halor = call(first_body, (s(n, 2 * d), s(2 * blk, 2 * d)), [VM] * 5)(
        h, pick, haloq, halor, packs[0]
    )

    def stages(rows):
        return [
            pltpu.VMEM((rows, 2 * d), BF),
            pltpu.VMEM((rows, 2 * d), BF),
            pltpu.VMEM((rows, 2 * d), F32),
        ]

    steps = layers * sections
    for step in range(steps):
        pack = packs[step // layers]
        if step + 1 == steps:
            out = call(
                last_body(step),
                s(2, n, d),
                [VM] * 8,
                stages(n) + [pltpu.VMEM((2, n, d), BF), pltpu.SemaphoreType.DMA((n // CHUNK,))],
                spaces=HB,
            )(h, m, pick, haloq, halor, dense, mask, pack)
            return out[None]
        nxt = packs[(step + 1) // layers]
        hs, q, r = call(
            send_body(step, step == 0),
            (s(2 * blk, 2 * d), s(blk, 2 * d), s(blk, 2 * d)),
            [VM] * 9,
            stages(2 * blk),
        )(hs, m, pick, haloq, halor, ds, ms, pack, nxt)
        far_halo, near_halo = halor, haloq
        haloq, halor = exchange(q, r)
        h, m = call(
            rows_body(step, step == 0), (s(n, 2 * d), s(n, 2 * d)), [VM] * 9, stages(n)
        )(h, m, pick, near_halo, far_halo, dense, mask, pack, nxt)


def solution(mesh):
    placed = (
        P(None, "dom", None),
        P("dom"),
        P("dom"),
        P("dom"),
        P("dom", None, None),
        P("dom"),
        P("dom"),
        P("section", None, None),
        P("section", None, None),
        P("section", None),
        P("section", None, None),
        P("section", None),
        P("section", None),
    )
    return jax.shard_map(
        shards,
        mesh=mesh,
        in_specs=placed,
        out_specs=P("section", None, "dom", None),
        check_vma=False,
    )
```

```python
import jax
import jax.numpy as jnp
from jax import lax
from jax.experimental import pallas as pl
from jax.experimental.pallas import tpu as pltpu
from jax.sharding import PartitionSpec as P


BF = jnp.bfloat16
F32 = jnp.float32
VM = pl.BlockSpec(memory_space=pltpu.VMEM)
SM = pl.BlockSpec(memory_space=pltpu.SMEM)
HB = pl.BlockSpec(memory_space=pltpu.HBM)
CHUNK = 256


def call(body, outs, ins, scratch=(), room=8, spaces=None):
    return pl.pallas_call(
        body,
        out_shape=outs,
        in_specs=ins,
        out_specs=spaces or jax.tree.map(lambda _: VM, outs),
        scratch_shapes=list(scratch),
        compiler_params=pltpu.CompilerParams(vmem_limit_bytes=room << 20),
    )


def in_hbm(*arrays):
    return [pltpu.with_memory_space_constraint(a, pltpu.HBM) for a in arrays]


def dot(a, b):
    return jnp.dot(a, b, preferred_element_type=F32)


def silu_of_twice(u):
    return (u + u * jnp.tanh(u)).astype(BF)


def twice(w):
    zero = jnp.zeros_like(w)
    return jnp.concatenate(
        [jnp.concatenate([w, zero], axis=1), jnp.concatenate([zero, w], axis=1)], axis=0
    )


def flags(cond, shape):
    return jnp.full(shape, jnp.where(cond, jnp.float32(1), jnp.float32(0)), F32).astype(BF)


def choose(pick, a, b):
    return a * pick[0] + b * pick[1]


def fetch_all(pairs, sem):
    copies = [pltpu.make_async_copy(src, dst, sem.at[i]) for i, (src, dst) in enumerate(pairs)]
    for copy in copies:
        copy.start()
    return copies


def parity():
    return lax.axis_index("dom") % 2


def to_partners(up, down):
    odd = parity() == 1
    return jnp.where(odd, down, up), jnp.where(odd, up, down)


def exchange_of(near, far, block, back):
    moved = jnp.where(far == near, 0, jnp.where(far == 0, near, far))

    def first(b):
        return jnp.where(b == near, 0, jnp.where(b == 0, near, b))

    def second(b):
        swapped = jnp.where(b == moved, 1, jnp.where(b == 1, moved, b))
        return jnp.where(moved == 0, b, swapped)

    return first(second(block)) if back else second(first(block))


def pack_body(wm, wh, bh, wo, bo, gain, out, am, ah, ao, vb, vo, vg, sem):
    d = wm.shape[2]
    for copy in fetch_all([(wm, am), (wh, ah), (wo, ao), (bh, vb), (bo, vo), (gain, vg)], sem):
        copy.wait()
    for i in range(2):
        out[i * d : (i + 1) * d] = (am[i].astype(F32) * 0.5).astype(BF)
        at = 2 * d + i * 2 * d
        out[at : at + 2 * d] = (ah[i].astype(F32) * 0.5).astype(BF)
        w = ao[i].astype(F32)
        at = 6 * d + i * d
        out[at : at + d] = (w - jnp.mean(w, axis=1, keepdims=True)).astype(BF)
    b = vo[...].astype(F32)
    b = b - jnp.mean(b, axis=1, keepdims=True)
    high = b.astype(BF).astype(F32)
    pad = jnp.zeros((8, d), F32)
    vectors = [vb[...].astype(F32) * 0.5, high, b - high, vg[...].astype(F32), pad]
    out[8 * d :] = jnp.concatenate(vectors, axis=0).astype(BF)


def blocks_body(count, up, down, rows, cols, x, adj, q, pay, sr, sk, xs, av, sem):
    blk, d = av.shape[1], av.shape[2]
    copies = fetch_all([(rows, sr), (cols, sk), (adj, av)], sem)
    blocks = to_partners(up[0], down[0])
    for i, block in enumerate(blocks):
        at = pl.ds(pl.multiple_of(block * blk, blk), blk)
        copies.append(pltpu.make_async_copy(x.at[:, at, :], xs.at[i], sem.at[3 + i]))
        copies[-1].start()
    for copy in copies:
        copy.wait()
    for i, (block, dst) in enumerate(zip(blocks, (q, pay))):
        row = block * blk + lax.broadcasted_iota(jnp.int32, (blk, d), 0)
        keep = jnp.where(row < count[0], jnp.float32(1), jnp.float32(0)).astype(BF)
        for m in range(2):
            dst[:blk, m * d : (m + 1) * d] = xs[i, m] * keep
    pay[blk:, d:] = keep
    far_col = jnp.where(parity() == 1, 9, 8)
    seen = jnp.zeros((blk, d), F32)
    for k in range(av.shape[0]):
        hit = (sr[k] == blocks[1]) & (sk[k] == far_col)
        seen = seen + av[k].astype(F32) * jnp.where(hit, jnp.float32(1), jnp.float32(0))
    pay[blk:, :d] = seen.astype(BF)


def prep_body(
    count, up, down, rows, cols, x, adj,
    h, dense, df, mask, pick, fpick, fsel,
    sr, sk, xv, av, acc, sem,
):
    n, d = xv.shape[1], xv.shape[2]
    blk = av.shape[1]
    last = n // blk
    copies = fetch_all([(rows, sr), (cols, sk), (x, xv), (adj, av)], sem)
    acc[...] = jnp.zeros_like(acc)
    wide = (blk, 2 * d)
    dom = lax.axis_index("dom")
    odd = parity() == 1
    alone = (dom == 0) | (dom == lax.axis_size("dom") - 1)
    pick[0] = flags(odd, wide)
    pick[1] = flags(jnp.logical_not(odd), wide)
    fpick[0] = flags(jnp.logical_not(odd | alone), wide)
    fpick[1] = flags(odd & jnp.logical_not(alone), wide)
    near, far = to_partners(up[0], down[0])
    fsel[0] = flags(near == far, wide)
    fsel[1] = flags(near != far, wide)
    copies[2].wait()
    for b in range(last):
        at = pl.ds(pl.multiple_of(exchange_of(near, far, b, False) * blk, blk), blk)
        row = b * blk + lax.broadcasted_iota(jnp.int32, wide, 0)
        keep = jnp.where(row < count[0], jnp.float32(1), jnp.float32(0)).astype(BF)
        mask[at, :] = keep
        both = [xv[m, b * blk : (b + 1) * blk] for m in range(2)]
        h[at, :] = jnp.concatenate(both, axis=1) * keep
    for copy in copies[:2] + copies[3:]:
        copy.wait()
    for k in range(av.shape[0]):
        c = sk[k]
        halo = jnp.where(odd, c, 2 * last + 1 - c)
        at = (
            exchange_of(near, far, sr[k], False),
            jnp.where(c < last, exchange_of(near, far, c, False), halo),
        )
        acc[at] = acc[at] + av[k].astype(F32)
    for r in range(last):
        for c in range(last + 2):
            dense[r * blk : (r + 1) * blk, c * blk : (c + 1) * blk] = acc[r, c].astype(BF)
    at = pl.ds(pl.multiple_of(jnp.where(near == far, 0, 1) * blk, blk), blk)
    df[...] = dense[at, :]


def message_weight(pack, i):
    d = pack.shape[1]
    return twice(pack[i * d : (i + 1) * d])


def first_body(h, pick, haloq, halor, pack, m, halo):
    w = message_weight(pack, 0)
    m[...] = silu_of_twice(dot(h[...], w))
    blk = haloq.shape[1]
    both = jnp.concatenate([choose(pick, haloq[0], haloq[1]), halor[:blk]], axis=0)
    halo[...] = silu_of_twice(dot(both, w))


def own_rows(h, m, halo, dense, mask):
    n = m.shape[0]

    def aggregate(at):
        return lambda: dot(dense[at, :n], m[...]) + dot(dense[at, n:], halo)

    chunks = [slice(r, r + CHUNK) for r in range(0, n, CHUNK)]
    return [(at, h.at[at], aggregate(at), mask.at[at]) for at in chunks]


def layer(chunks, pack, i, agg, hidden, c):
    d = pack.shape[1]
    wh = pack[2 * d + i * 2 * d : 2 * d + (i + 1) * 2 * d]
    wo = twice(pack[6 * d + i * d : 6 * d + (i + 1) * d])
    v = pack[8 * d :].astype(F32)

    def row(j):
        r = v[j + i : j + i + 1]
        return jnp.concatenate([r, r], axis=1)

    for at, _, aggregate, _ in chunks:
        agg[at] = aggregate().astype(BF)
    b = row(0)
    for at, h, _, _ in chunks:
        pre = [
            dot(jnp.concatenate([h[:, s : s + d], agg[at, s : s + d]], axis=1), wh) for s in (0, d)
        ]
        hidden[at] = silu_of_twice(jnp.concatenate(pre, axis=1) + b)
    b = row(2) + row(4)
    for at, _, _, _ in chunks:
        c[at] = dot(hidden[at], wo) + b
    mean = twice(jnp.full((d, d), 1.0 / d, BF))
    gain = row(6)
    for at, h, _, mask in chunks:
        now = c[at]
        var = dot((now * now).astype(BF), mean)
        new = (h[...].astype(F32) + now * lax.rsqrt(var + 1e-05) * gain).astype(BF) * mask[...]
        yield at, new


def send_messages(new_h, new_m, outq, nxt, i):
    w = message_weight(nxt, i)
    for r in range(0, new_m.shape[0], CHUNK):
        at = slice(r, r + CHUNK)
        out = silu_of_twice(dot(new_h[at], w))
        new_m[at] = out
        if r == 0:
            outq[...] = out[: outq.shape[0]]


def far_block(fsel, ref, blk):
    return choose(fsel, ref[:blk], ref[blk : 2 * blk])


def second_body(step, given, tail):
    def body(h, m, pick, haloq, halor, dense, df, mask, fsel, pack, nxt, *rest):
        new_h, new_m, outq = rest[:3]
        agg, hidden, c = rest[-3:]
        blk = outq.shape[0]
        if given:
            halo = halor[...]
        else:
            near = choose(pick, haloq[0], haloq[1])
            halo = jnp.concatenate([near, halor[...]], axis=0)
        for at, new in layer(own_rows(h, m, halo, dense, mask), pack, step % 2, agg, hidden, c):
            new_h[at] = new
        send_messages(new_h, new_m, outq, nxt, (step + 1) % 2)
        if tail:
            rest[3][...] = far_block(fsel, new_m, blk)
        else:
            rest[3][...] = far_block(fsel, new_h, blk)
            rest[4][...] = dot(df[:, : new_m.shape[0]], new_m[...])

    return body


def pay_body(pick, haloq, df, far_h, part, pay):
    blk = far_h.shape[0]
    n = df.shape[1] - 2 * blk
    near = choose(pick, haloq[0], haloq[1])
    pay[:blk] = far_h[...]
    pay[blk:] = (part[...] + dot(df[:, n : n + blk], near)).astype(BF)


def first_of_two_body(step):
    def body(h, m, pick, haloq, fpick, far, dense, mask, fsel, seen, pack, nxt, *rest):
        new_h, new_m, outq, far_m, agg, hidden, c, hx, mx = rest
        n = m.shape[0]
        blk, d2 = hx.shape
        d = d2 // 2
        hx[...] = choose(fpick, far[0, :blk], far[1, :blk])
        part = choose(fpick, far[0, blk:], far[1, blk:])
        view = seen[blk:]
        mx[...] = jnp.concatenate([view[:, d:], view[:, d:]], axis=1)
        theirs = silu_of_twice(dot(hx[...], message_weight(pack, step % 2)))
        halo = jnp.concatenate([choose(pick, haloq[0], haloq[1]), theirs], axis=0)
        mine = far_block(fsel, m, blk)
        chunks = own_rows(h, m, halo, dense, mask)
        chunks.append(
            (slice(n, n + blk), hx, lambda: part.astype(F32) + dot(view[:, :d], mine), mx)
        )
        for at, new in layer(chunks, pack, step % 2, agg, hidden, c):
            if at.start < n:
                new_h[at] = new
            else:
                hx[...] = new
        send_messages(new_h, new_m, outq, nxt, (step + 1) % 2)
        far_m[...] = silu_of_twice(dot(hx[...], message_weight(nxt, (step + 1) % 2)))

    return body


def last_body(step):
    def body(h, m, pick, haloq, halor, dense, mask, pack, up, down, out, *rest):
        agg, hidden, c, stage, sem = rest
        d = pack.shape[1]
        blk = halor.shape[0]
        halo = jnp.concatenate([choose(pick, haloq[0], haloq[1]), halor[...]], axis=0)
        near, far = to_partners(up[0], down[0])
        copies = []
        for at, new in layer(own_rows(h, m, halo, dense, mask), pack, step % 2, agg, hidden, c):
            stage[0, at] = new[:, :d]
            stage[1, at] = new[:, d:]
            for b in range(at.start // blk, at.stop // blk):
                to = pl.multiple_of(exchange_of(near, far, b, True) * blk, blk)
                copies.append(
                    pltpu.make_async_copy(
                        stage.at[:, b * blk : (b + 1) * blk, :],
                        out.at[:, pl.ds(to, blk), :],
                        sem.at[b],
                    )
                )
                copies[-1].start()
        for copy in copies:
            copy.wait()

    return body


def shards(
    features,
    counts,
    row_blocks,
    col_blocks,
    adjacency,
    send_up,
    send_down,
    w_message,
    w_hidden,
    b_hidden,
    w_out,
    b_out,
    gain,
):
    n, d = features.shape[1:]
    blk = adjacency.shape[1]
    doms = lax.axis_size("dom")
    sections = lax.axis_size("section")
    layers = w_message.shape[0]
    steps = layers * sections
    near_pairs = [[i, i + 1] for i in range(0, doms, 2)]
    far_pairs = [[i, i + 1] for i in range(1, doms - 1, 2)]
    across = [(a, b) for a, b in far_pairs] + [(b, a) for a, b in far_pairs]
    far_pairs = far_pairs + [[0, doms - 1]]

    def s(*shape, dtype=BF):
        return jax.ShapeDtypeStruct(shape, dtype)

    def near_gather(q):
        return lax.all_gather(q, "dom", axis_index_groups=near_pairs)

    def fetch(own, k):
        return lax.ppermute(own, "section", [(i, i + k) for i in range(sections - k)])

    def integers(*sizes):
        return [pltpu.SMEM((k,), jnp.int32) for k in sizes]

    wide = s(blk, 2 * d)
    rows = s(n, 2 * d)
    two = s(2, blk, 2 * d)
    span = n + 2 * blk
    count_k = adjacency.shape[0]
    vec = pltpu.VMEM((layers, d), BF)
    weights = in_hbm(w_message, w_hidden, b_hidden, w_out, b_out, gain)
    own = call(
        pack_body,
        s(layers * 4 * d + 16, d),
        [HB] * 6,
        [
            pltpu.VMEM((layers, d, d), BF),
            pltpu.VMEM((layers, 2 * d, d), BF),
            pltpu.VMEM((layers, d, d), BF),
            vec,
            vec,
            vec,
            pltpu.SemaphoreType.DMA((6,)),
        ],
    )(*weights)
    packs = [fetch(own, sections - 1)]
    graph = [counts, send_up, send_down, *in_hbm(row_blocks, col_blocks, features, adjacency)]
    q, pay = call(
        blocks_body,
        (wide, s(2 * blk, 2 * d)),
        [SM] * 3 + [HB] * 4,
        integers(count_k, count_k)
        + [
            pltpu.VMEM((2, 2, blk, d), BF),
            pltpu.VMEM(adjacency.shape, BF),
            pltpu.SemaphoreType.DMA((5,)),
        ],
    )(*graph)
    seen = lax.ppermute(pay, "dom", across)
    prep = call(
        prep_body,
        (rows, s(n, span), s(blk, span), rows, two, two, two),
        [SM] * 3 + [HB] * 4,
        integers(count_k, count_k)
        + [
            pltpu.VMEM(features.shape, BF),
            pltpu.VMEM(adjacency.shape, BF),
            pltpu.VMEM((n // blk, n // blk + 2, blk, blk), F32),
            pltpu.SemaphoreType.DMA((4,)),
        ],
        16,
    )
    h, dense, df, mask, pick, fpick, fsel = prep(*graph)
    q, pick = lax.optimization_barrier((q, pick))
    haloq = near_gather(q)
    later, haloq = lax.optimization_barrier((own, haloq))
    packs += [fetch(later, k) for k in range(sections - 2, 0, -1)] + [own]
    m, halo = call(first_body, (rows, s(2 * blk, 2 * d)), [VM] * 5)(h, pick, haloq, seen, packs[0])

    def stages(k):
        return [
            pltpu.VMEM((k, 2 * d), BF),
            pltpu.VMEM((k, 2 * d), BF),
            pltpu.VMEM((k, 2 * d), F32),
        ]

    def second(step, halo, given):
        tail = step + 2 == steps
        outs = (rows, rows, wide, wide) + (() if tail else (s(blk, 2 * d, dtype=F32),))
        return call(second_body(step, given, tail), outs, [VM] * 11, stages(n))(
            h, m, pick, haloq, halo, dense, df, mask, fsel,
            packs[step // layers], packs[(step + 1) // layers],
        )

    h, m, q, *far = second(0, halo, True)
    for step in range(1, steps - 1, 2):
        haloq = near_gather(q)
        pay = call(pay_body, s(2 * blk, 2 * d), [VM] * 5)(pick, haloq, df, *far)
        asked = lax.all_gather(pay, "dom", axis_index_groups=far_pairs)
        h, m, q, far_m = call(
            first_of_two_body(step),
            (rows, rows, wide, wide),
            [VM] * 12,
            stages(n + blk) + [pltpu.VMEM((blk, 2 * d), BF)] * 2,
        )(
            h, m, pick, haloq, fpick, asked, dense, mask, fsel, seen,
            packs[step // layers], packs[(step + 1) // layers],
        )
        haloq = near_gather(q)
        h, m, q, *far = second(step + 1, far_m, False)
    far_m = lax.ppermute(far[0], "dom", across)
    haloq = near_gather(q)
    out = call(
        last_body(steps - 1),
        s(2, n, d),
        [VM] * 8 + [SM] * 2,
        stages(n)
        + [pltpu.VMEM((2, n, d), BF)]
        + [pltpu.SemaphoreType.DMA((n // blk,))],
        spaces=HB,
    )(h, m, pick, haloq, far_m, dense, mask, packs[-1], send_up, send_down)
    return out[None]


def solution(mesh):
    placed = (
        P(None, "dom", None),
        P("dom"),
        P("dom"),
        P("dom"),
        P("dom", None, None),
        P("dom"),
        P("dom"),
        P("section", None, None),
        P("section", None, None),
        P("section", None),
        P("section", None, None),
        P("section", None),
        P("section", None),
    )
    return jax.shard_map(
        shards,
        mesh=mesh,
        in_specs=placed,
        out_specs=P("section", None, "dom", None),
        check_vma=False,
    )
```

```python
import jax
import jax.numpy as jnp
from jax import lax
from jax.experimental import pallas as pl
from jax.experimental.pallas import tpu as pltpu
from jax.sharding import PartitionSpec as P


BF = jnp.bfloat16
F32 = jnp.float32
VM = pl.BlockSpec(memory_space=pltpu.VMEM)
HB = pl.BlockSpec(memory_space=pltpu.HBM)
CHUNK = 256


def call(body, outs, ins, scratch=(), room=8, spaces=None):
    return pl.pallas_call(
        body,
        out_shape=outs,
        in_specs=ins,
        out_specs=spaces or jax.tree.map(lambda _: VM, outs),
        scratch_shapes=list(scratch),
        compiler_params=pltpu.CompilerParams(vmem_limit_bytes=room << 20),
    )


def in_hbm(*arrays):
    return [pltpu.with_memory_space_constraint(a, pltpu.HBM) for a in arrays]


def dot(a, b):
    return jnp.dot(a, b, preferred_element_type=F32)


def silu_of_twice(u):
    return (u + u * jnp.tanh(u)).astype(BF)


def twice(w):
    zero = jnp.zeros_like(w)
    return jnp.concatenate(
        [jnp.concatenate([w, zero], axis=1), jnp.concatenate([zero, w], axis=1)], axis=0
    )


def flags(cond, shape):
    return jnp.full(shape, jnp.where(cond, jnp.float32(1), jnp.float32(0)), F32).astype(BF)


def choose(pick, a, b):
    return a * pick[0] + b * pick[1]


def fetch_all(pairs, sem):
    copies = [pltpu.make_async_copy(src, dst, sem.at[i]) for i, (src, dst) in enumerate(pairs)]
    for copy in copies:
        copy.start()
    return copies


def parity():
    return lax.axis_index("dom") % 2


def to_partners(up, down):
    odd = parity() == 1
    return jnp.where(odd, down, up), jnp.where(odd, up, down)


def exchange_of(near, far, block, back):
    moved = jnp.where(far == near, 0, jnp.where(far == 0, near, far))

    def first(b):
        return jnp.where(b == near, 0, jnp.where(b == 0, near, b))

    def second(b):
        swapped = jnp.where(b == moved, 1, jnp.where(b == 1, moved, b))
        return jnp.where(moved == 0, b, swapped)

    return first(second(block)) if back else second(first(block))


def pack_body(wm, wh, bh, wo, bo, gain, out, am, ah, ao, vb, vo, vg, sem):
    d = wm.shape[2]
    for copy in fetch_all([(wm, am), (wh, ah), (wo, ao), (bh, vb), (bo, vo), (gain, vg)], sem):
        copy.wait()
    for i in range(2):
        out[i * d : (i + 1) * d] = (am[i].astype(F32) * 0.5).astype(BF)
        at = 2 * d + i * 2 * d
        out[at : at + 2 * d] = (ah[i].astype(F32) * 0.5).astype(BF)
        w = ao[i].astype(F32)
        at = 6 * d + i * d
        out[at : at + d] = (w - jnp.mean(w, axis=1, keepdims=True)).astype(BF)
    b = vo[...].astype(F32)
    b = b - jnp.mean(b, axis=1, keepdims=True)
    high = b.astype(BF).astype(F32)
    pad = jnp.zeros((8, d), F32)
    vectors = [vb[...].astype(F32) * 0.5, high, b - high, vg[...].astype(F32), pad]
    out[8 * d :] = jnp.concatenate(vectors, axis=0).astype(BF)


def blocks_body(ints, rows, cols, x, adj, q, pay, si, sr, sk, xs, av, sem):
    blk, d = av.shape[1], av.shape[2]
    copies = fetch_all([(ints, si), (rows, sr), (cols, sk), (adj, av)], sem)
    copies[0].wait()
    blocks = to_partners(si[1], si[2])
    for i, block in enumerate(blocks):
        at = pl.ds(pl.multiple_of(block * blk, blk), blk)
        copies.append(pltpu.make_async_copy(x.at[:, at, :], xs.at[i], sem.at[4 + i]))
        copies[-1].start()
    for copy in copies[1:]:
        copy.wait()
    for i, (block, dst) in enumerate(zip(blocks, (q, pay))):
        row = block * blk + lax.broadcasted_iota(jnp.int32, (blk, d), 0)
        keep = jnp.where(row < si[0], jnp.float32(1), jnp.float32(0)).astype(BF)
        for m in range(2):
            dst[:blk, m * d : (m + 1) * d] = xs[i, m] * keep
        dst[blk:, d:] = keep
        col = jnp.where(parity() == i, 9, 8)
        seen = jnp.zeros((blk, d), F32)
        for k in range(av.shape[0]):
            hit = (sr[k] == block) & (sk[k] == col)
            seen = seen + av[k].astype(F32) * jnp.where(hit, jnp.float32(1), jnp.float32(0))
        dst[blk:, :d] = seen.astype(BF)


def prep_body(
    ints, rows, cols, x, adj,
    h, dense, df, mask, pick, fpick, fsel,
    si, sr, sk, xv, av, acc, sem,
):
    n, d = xv.shape[1], xv.shape[2]
    blk = av.shape[1]
    last = n // blk
    copies = fetch_all([(ints, si), (rows, sr), (cols, sk), (x, xv), (adj, av)], sem)
    acc[...] = jnp.zeros_like(acc)
    wide = (blk, 2 * d)
    dom = lax.axis_index("dom")
    odd = parity() == 1
    alone = (dom == 0) | (dom == lax.axis_size("dom") - 1)
    pick[0] = flags(odd, wide)
    pick[1] = flags(jnp.logical_not(odd), wide)
    fpick[0] = flags(jnp.logical_not(odd | alone), wide)
    fpick[1] = flags(odd & jnp.logical_not(alone), wide)
    copies[0].wait()
    near, far = to_partners(si[1], si[2])
    fsel[0] = flags(near == far, wide)
    fsel[1] = flags(near != far, wide)
    copies[3].wait()
    for b in range(last):
        at = pl.ds(pl.multiple_of(exchange_of(near, far, b, False) * blk, blk), blk)
        row = b * blk + lax.broadcasted_iota(jnp.int32, wide, 0)
        keep = jnp.where(row < si[0], jnp.float32(1), jnp.float32(0)).astype(BF)
        mask[at, :] = keep
        both = [xv[m, b * blk : (b + 1) * blk] for m in range(2)]
        h[at, :] = jnp.concatenate(both, axis=1) * keep
    for copy in copies[1:3] + copies[4:]:
        copy.wait()
    for k in range(av.shape[0]):
        c = sk[k]
        halo = jnp.where(odd, c, 2 * last + 1 - c)
        at = (
            exchange_of(near, far, sr[k], False),
            jnp.where(c < last, exchange_of(near, far, c, False), halo),
        )
        acc[at] = acc[at] + av[k].astype(F32)
    for r in range(last):
        for c in range(last + 2):
            dense[r * blk : (r + 1) * blk, c * blk : (c + 1) * blk] = acc[r, c].astype(BF)
    at = pl.ds(pl.multiple_of(jnp.where(near == far, 0, 1) * blk, blk), blk)
    df[...] = dense[at, :]


def message_weight(pack, i):
    d = pack.shape[1]
    return twice(pack[i * d : (i + 1) * d])


def first_body(h, pick, haloq, halor, pack, m, halo, nseen):
    w = message_weight(pack, 0)
    m[...] = silu_of_twice(dot(h[...], w))
    blk = nseen.shape[0]
    both = jnp.concatenate([choose(pick, haloq[0, :blk], haloq[1, :blk]), halor[:blk]], axis=0)
    halo[...] = silu_of_twice(dot(both, w))
    nseen[...] = choose(pick, haloq[0, blk:], haloq[1, blk:])


def own_rows(h, m, halo, dense, mask):
    n = m.shape[0]

    def aggregate(at):
        return lambda: dot(dense[at, :n], m[...]) + dot(dense[at, n:], halo)

    chunks = [slice(r, r + CHUNK) for r in range(0, n, CHUNK)]
    return [(at, h.at[at], aggregate(at), mask.at[at]) for at in chunks]


def layer(chunks, pack, i, agg, hidden, c):
    d = pack.shape[1]
    wh = pack[2 * d + i * 2 * d : 2 * d + (i + 1) * 2 * d]
    wo = twice(pack[6 * d + i * d : 6 * d + (i + 1) * d])
    v = pack[8 * d :].astype(F32)

    def row(j):
        r = v[j + i : j + i + 1]
        return jnp.concatenate([r, r], axis=1)

    for at, _, aggregate, _ in chunks:
        agg[at] = aggregate().astype(BF)
    b = row(0)
    for at, h, _, _ in chunks:
        pre = [
            dot(jnp.concatenate([h[:, s : s + d], agg[at, s : s + d]], axis=1), wh) for s in (0, d)
        ]
        hidden[at] = silu_of_twice(jnp.concatenate(pre, axis=1) + b)
    b = row(2) + row(4)
    for at, _, _, _ in chunks:
        c[at] = dot(hidden[at], wo) + b
    mean = twice(jnp.full((d, d), 1.0 / d, BF))
    gain = row(6)
    for at, h, _, mask in chunks:
        now = c[at]
        var = dot((now * now).astype(BF), mean)
        new = (h[...].astype(F32) + now * lax.rsqrt(var + 1e-05) * gain).astype(BF) * mask[...]
        yield at, new


def send_messages(new_h, new_m, nxt, i):
    w = message_weight(nxt, i)
    for r in range(0, new_m.shape[0], CHUNK):
        at = slice(r, r + CHUNK)
        new_m[at] = silu_of_twice(dot(new_h[at], w))


def far_block(fsel, ref, blk):
    return choose(fsel, ref[:blk], ref[blk : 2 * blk])


def start_body(step):
    def body(h, m, halo, dense, df, mask, fsel, pack, nxt, new_h, new_m, outq, far_h, part, *rest):
        blk = outq.shape[0]
        for at, new in layer(own_rows(h, m, halo[...], dense, mask), pack, step % 2, *rest):
            new_h[at] = new
        send_messages(new_h, new_m, nxt, (step + 1) % 2)
        outq[...] = new_m[:blk]
        far_h[...] = far_block(fsel, new_h, blk)
        part[...] = dot(df[:, : new_m.shape[0]], new_m[...])

    return body


def pay_body(pick, haloq, df, far_h, part, pay, near_m):
    blk = far_h.shape[0]
    n = df.shape[1] - 2 * blk
    near = choose(pick, haloq[0], haloq[1])
    near_m[...] = near
    pay[:blk] = far_h[...]
    pay[blk:] = (part[...] + dot(df[:, n : n + blk], near)).astype(BF)


def partner_layer(h, m, given, pick, seen, mine, other, is_far, dense, mask, pack, i, new_h, rest):
    agg, hidden, c, hx, mx = rest
    n = m.shape[0]
    blk, d2 = hx.shape
    d = d2 // 2
    hx[...] = choose(pick, given[0, :blk], given[1, :blk])
    part = choose(pick, given[0, blk:], given[1, blk:])
    mx[...] = jnp.concatenate([seen[:, d:], seen[:, d:]], axis=1)
    theirs = silu_of_twice(dot(hx[...], message_weight(pack, i)))
    halo = jnp.concatenate([other, theirs] if is_far else [theirs, other], axis=0)
    chunks = own_rows(h, m, halo, dense, mask)
    chunks.append(
        (slice(n, n + blk), hx, lambda: part.astype(F32) + dot(seen[:, :d], mine), mx)
    )
    for at, new in layer(chunks, pack, i, agg, hidden, c):
        if at.start < n:
            new_h[at] = new
        else:
            hx[...] = new


def far_layer_body(step):
    def body(h, m, near_m, fpick, far, dense, mask, fsel, seen, pack, nxt, *rest):
        new_h, new_m, pay, far_m = rest[:4]
        rest = rest[4:]
        n, blk = m.shape[0], far_m.shape[0]
        mine = far_block(fsel, m, blk)
        partner_layer(
            h, m, far, fpick, seen[blk:], mine, near_m[...], True, dense, mask, pack, step % 2,
            new_h, rest,
        )
        send_messages(new_h, new_m, nxt, (step + 1) % 2)
        theirs = silu_of_twice(dot(rest[3][...], message_weight(nxt, (step + 1) % 2)))
        far_m[...] = theirs
        pay[:blk] = new_h[:blk]
        part = dot(dense[:blk, :n], new_m[...]) + dot(dense[:blk, n + blk :], theirs)
        pay[blk:] = part.astype(BF)

    return body


def near_layer_body(step, tail):
    def body(h, m, far_m, pick, near, dense, df, mask, fsel, nseen, pack, nxt, *rest):
        new_h, new_m, pay, near_m = rest[:4]
        rest = rest[4:]
        n, blk = m.shape[0], near_m.shape[0]
        partner_layer(
            h, m, near, pick, nseen[...], m[:blk], far_m[...], False, dense, mask, pack, step % 2,
            new_h, rest,
        )
        send_messages(new_h, new_m, nxt, (step + 1) % 2)
        theirs = silu_of_twice(dot(rest[3][...], message_weight(nxt, (step + 1) % 2)))
        near_m[...] = theirs
        if tail:
            pay[...] = far_block(fsel, new_m, blk)
        else:
            pay[:blk] = far_block(fsel, new_h, blk)
            part = dot(df[:, :n], new_m[...]) + dot(df[:, n : n + blk], theirs)
            pay[blk:] = part.astype(BF)

    return body


def last_body(step):
    def body(h, m, near_m, fpick, far, dense, mask, pack, ints, out, agg, hidden, c, stage, si, sem):
        d = pack.shape[1]
        blk = near_m.shape[0]
        (asked,) = fetch_all([(ints, si)], sem)
        halo = jnp.concatenate([near_m[...], choose(fpick, far[0], far[1])], axis=0)
        asked.wait()
        near, far = to_partners(si[1], si[2])
        copies = []
        for at, new in layer(own_rows(h, m, halo, dense, mask), pack, step % 2, agg, hidden, c):
            stage[0, at] = new[:, :d]
            stage[1, at] = new[:, d:]
            for b in range(at.start // blk, at.stop // blk):
                to = pl.multiple_of(exchange_of(near, far, b, True) * blk, blk)
                copies.append(
                    pltpu.make_async_copy(
                        stage.at[:, b * blk : (b + 1) * blk, :],
                        out.at[:, pl.ds(to, blk), :],
                        sem.at[1 + b],
                    )
                )
                copies[-1].start()
        for copy in copies:
            copy.wait()

    return body


def shards(
    features,
    counts,
    row_blocks,
    col_blocks,
    adjacency,
    send_up,
    send_down,
    w_message,
    w_hidden,
    b_hidden,
    w_out,
    b_out,
    gain,
):
    n, d = features.shape[1:]
    blk = adjacency.shape[1]
    doms = lax.axis_size("dom")
    sections = lax.axis_size("section")
    layers = w_message.shape[0]
    steps = layers * sections
    near_pairs = [[i, i + 1] for i in range(0, doms, 2)]
    far_pairs = [[i, i + 1] for i in range(1, doms - 1, 2)]
    across = [(a, b) for a, b in far_pairs] + [(b, a) for a, b in far_pairs]
    far_pairs = far_pairs + [[0, doms - 1]]

    def s(*shape, dtype=BF):
        return jax.ShapeDtypeStruct(shape, dtype)

    def near_gather(q):
        return lax.all_gather(q, "dom", axis_index_groups=near_pairs)

    def fetch(own, k):
        return lax.ppermute(own, "section", [(i, i + k) for i in range(sections - k)])

    def integers(*sizes):
        return [pltpu.SMEM((k,), jnp.int32) for k in sizes]

    def far_gather(q, step):
        groups = []
        for section in range(sections):
            begun = layers * (sections - 1 - section) <= step + 1
            groups += [
                [section * doms + i for i in pair] for pair in (far_pairs if begun else near_pairs)
            ]
        return lax.all_gather(q, ("section", "dom"), axis_index_groups=groups)

    wide = s(blk, 2 * d)
    both = s(2 * blk, 2 * d)
    rows = s(n, 2 * d)
    two = s(2, blk, 2 * d)
    span = n + 2 * blk
    count_k = adjacency.shape[0]
    vec = pltpu.VMEM((layers, d), BF)
    weights = in_hbm(w_message, w_hidden, b_hidden, w_out, b_out, gain)
    own = call(
        pack_body,
        s(layers * 4 * d + 16, d),
        [HB] * 6,
        [
            pltpu.VMEM((layers, d, d), BF),
            pltpu.VMEM((layers, 2 * d, d), BF),
            pltpu.VMEM((layers, d, d), BF),
            vec,
            vec,
            vec,
            pltpu.SemaphoreType.DMA((6,)),
        ],
    )(*weights)
    packs = [fetch(own, sections - 1)]
    ints = jnp.concatenate([counts, send_up, send_down, jnp.zeros((125,), jnp.int32)])
    graph = in_hbm(ints, row_blocks, col_blocks, features, adjacency)
    q, pay = call(
        blocks_body,
        (both, both),
        [HB] * 5,
        integers(128, count_k, count_k)
        + [
            pltpu.VMEM((2, 2, blk, d), BF),
            pltpu.VMEM(adjacency.shape, BF),
            pltpu.SemaphoreType.DMA((6,)),
        ],
    )(*graph)
    seen = lax.ppermute(pay, "dom", across)
    prep = call(
        prep_body,
        (rows, s(n, span), s(blk, span), rows, two, two, two),
        [HB] * 5,
        integers(128, count_k, count_k)
        + [
            pltpu.VMEM(features.shape, BF),
            pltpu.VMEM(adjacency.shape, BF),
            pltpu.VMEM((n // blk, n // blk + 2, blk, blk), F32),
            pltpu.SemaphoreType.DMA((5,)),
        ],
        16,
    )
    h, dense, df, mask, pick, fpick, fsel = prep(*graph)
    q, pick = lax.optimization_barrier((q, pick))
    haloq = near_gather(q)
    later, haloq = lax.optimization_barrier((own, haloq))
    packs += [fetch(later, k) for k in range(sections - 2, 0, -1)] + [own]
    m, halo, nseen = call(first_body, (rows, both, wide), [VM] * 5)(h, pick, haloq, seen, packs[0])

    def stages(k):
        return [
            pltpu.VMEM((k, 2 * d), BF),
            pltpu.VMEM((k, 2 * d), BF),
            pltpu.VMEM((k, 2 * d), F32),
        ]

    def weights_at(step):
        return packs[step // layers], packs[(step + 1) // layers]

    h, m, q, far_h, part = call(
        start_body(0), (rows, rows, wide, wide, s(blk, 2 * d, dtype=F32)), [VM] * 9, stages(n)
    )(h, m, halo, dense, df, mask, fsel, *weights_at(0))
    pay, near_m = call(pay_body, (both, wide), [VM] * 5)(pick, near_gather(q), df, far_h, part)
    more = stages(n + blk) + [pltpu.VMEM((blk, 2 * d), BF)] * 2
    for step in range(1, steps - 1, 2):
        asked = far_gather(pay, step)
        h, m, pay, far_m = call(
            far_layer_body(step), (rows, rows, both, wide), [VM] * 11, more
        )(h, m, near_m, fpick, asked, dense, mask, fsel, seen, *weights_at(step))
        asked = near_gather(pay)
        step += 1
        tail = step + 2 == steps
        h, m, pay, near_m = call(
            near_layer_body(step, tail), (rows, rows, wide if tail else both, wide), [VM] * 12, more
        )(h, m, far_m, pick, asked, dense, df, mask, fsel, nseen, *weights_at(step))
    out = call(
        last_body(steps - 1),
        s(2, n, d),
        [VM] * 8 + [HB],
        stages(n)
        + [pltpu.VMEM((2, n, d), BF)]
        + integers(128)
        + [pltpu.SemaphoreType.DMA((1 + n // blk,))],
        spaces=HB,
    )(h, m, near_m, fpick, far_gather(pay, steps - 1), dense, mask, packs[-1], graph[0])
    return out[None]


def solution(mesh):
    placed = (
        P(None, "dom", None),
        P("dom"),
        P("dom"),
        P("dom"),
        P("dom", None, None),
        P("dom"),
        P("dom"),
        P("section", None, None),
        P("section", None, None),
        P("section", None),
        P("section", None, None),
        P("section", None),
        P("section", None),
    )
    return jax.shard_map(
        shards,
        mesh=mesh,
        in_specs=placed,
        out_specs=P("section", None, "dom", None),
        check_vma=False,
    )
```

```python
import jax
import jax.numpy as jnp
from jax import lax
from jax.experimental import pallas as pl
from jax.experimental.pallas import tpu as pltpu
from jax.sharding import PartitionSpec as P


BF = jnp.bfloat16
F32 = jnp.float32
VM = pl.BlockSpec(memory_space=pltpu.VMEM)
SM = pl.BlockSpec(memory_space=pltpu.SMEM)
HB = pl.BlockSpec(memory_space=pltpu.HBM)
CHUNK = 512
LOCAL_FIRST = True


def call(body, outs, ins, scratch=(), room=8, spaces=None):
    return pl.pallas_call(
        body,
        out_shape=outs,
        in_specs=ins,
        out_specs=spaces or jax.tree.map(lambda _: VM, outs),
        scratch_shapes=list(scratch),
        compiler_params=pltpu.CompilerParams(vmem_limit_bytes=room << 20),
    )


def in_hbm(*arrays):
    return [pltpu.with_memory_space_constraint(a, pltpu.HBM) for a in arrays]


def dot(a, b):
    return jnp.dot(a, b, preferred_element_type=F32)


def silu_of_twice(u):
    return (u + u * jnp.tanh(u)).astype(BF)


def twice(w):
    zero = jnp.zeros_like(w)
    return jnp.concatenate(
        [jnp.concatenate([w, zero], axis=1), jnp.concatenate([zero, w], axis=1)], axis=0
    )


def flags(cond, shape):
    return jnp.full(shape, jnp.where(cond, jnp.float32(1), jnp.float32(0)), F32).astype(BF)


def choose(pick, a, b):
    return a * pick[0] + b * pick[1]


def fetch_all(pairs, sem):
    copies = [pltpu.make_async_copy(src, dst, sem.at[i]) for i, (src, dst) in enumerate(pairs)]
    for copy in copies:
        copy.start()
    return copies


def parity():
    return lax.axis_index("dom") % 2


def to_partners(up, down):
    odd = parity() == 1
    return jnp.where(odd, down, up), jnp.where(odd, up, down)


def exchange_of(near, far, block, back):
    moved = jnp.where(far == near, 0, jnp.where(far == 0, near, far))

    def first(b):
        return jnp.where(b == near, 0, jnp.where(b == 0, near, b))

    def second(b):
        swapped = jnp.where(b == moved, 1, jnp.where(b == 1, moved, b))
        return jnp.where(moved == 0, b, swapped)

    return first(second(block)) if back else second(first(block))


def pack_body(wm, wh, bh, wo, bo, gain, out, am, ah, ao, vb, vo, vg, sem):
    d = wm.shape[2]
    for copy in fetch_all([(wm, am), (wh, ah), (wo, ao), (bh, vb), (bo, vo), (gain, vg)], sem):
        copy.wait()
    for i in range(2):
        out[i * d : (i + 1) * d] = (am[i].astype(F32) * 0.5).astype(BF)
        at = 2 * d + i * 2 * d
        out[at : at + 2 * d] = (ah[i].astype(F32) * 0.5).astype(BF)
        w = ao[i].astype(F32)
        at = 6 * d + i * d
        out[at : at + d] = (w - jnp.mean(w, axis=1, keepdims=True)).astype(BF)
    b = vo[...].astype(F32)
    b = b - jnp.mean(b, axis=1, keepdims=True)
    high = b.astype(BF).astype(F32)
    pad = jnp.zeros((8, d), F32)
    vectors = [vb[...].astype(F32) * 0.5, high, b - high, vg[...].astype(F32), pad]
    out[8 * d :] = jnp.concatenate(vectors, axis=0).astype(BF)


def blocks_body(count, up, down, rows, cols, x, adj, q, pay, sr, sk, xs, av, sem):
    blk, d = av.shape[1], av.shape[2]
    copies = fetch_all([(rows, sr), (cols, sk), (adj, av)], sem)
    blocks = to_partners(up[0], down[0])
    for i, block in enumerate(blocks):
        at = pl.ds(pl.multiple_of(block * blk, blk), blk)
        copies.append(pltpu.make_async_copy(x.at[:, at, :], xs.at[i], sem.at[3 + i]))
        copies[-1].start()
    for copy in copies:
        copy.wait()
    for i, (block, dst) in enumerate(zip(blocks, (q, pay))):
        row = block * blk + lax.broadcasted_iota(jnp.int32, (blk, d), 0)
        keep = jnp.where(row < count[0], jnp.float32(1), jnp.float32(0)).astype(BF)
        for m in range(2):
            dst[:blk, m * d : (m + 1) * d] = xs[i, m] * keep
        dst[blk:, d:] = keep
        col = jnp.where(parity() == i, 9, 8)
        seen = jnp.zeros((blk, d), F32)
        for k in range(av.shape[0]):
            hit = (sr[k] == block) & (sk[k] == col)
            seen = seen + av[k].astype(F32) * jnp.where(hit, jnp.float32(1), jnp.float32(0))
        dst[blk:, :d] = seen.astype(BF)


def prep_body(
    count, up, down, rows, cols, x, adj,
    h, dense, df, mask, pick, fpick, fsel,
    sr, sk, xv, av, acc, sem,
):
    n, d = xv.shape[1], xv.shape[2]
    blk = av.shape[1]
    last = n // blk
    copies = fetch_all([(rows, sr), (cols, sk), (x, xv), (adj, av)], sem)
    acc[...] = jnp.zeros_like(acc)
    wide = (blk, 2 * d)
    dom = lax.axis_index("dom")
    odd = parity() == 1
    alone = (dom == 0) | (dom == lax.axis_size("dom") - 1)
    pick[0] = flags(odd, wide)
    pick[1] = flags(jnp.logical_not(odd), wide)
    fpick[0] = flags(jnp.logical_not(odd | alone), wide)
    fpick[1] = flags(odd & jnp.logical_not(alone), wide)
    near, far = to_partners(up[0], down[0])
    fsel[0] = flags(near == far, wide)
    fsel[1] = flags(near != far, wide)
    copies[2].wait()
    for b in range(last):
        at = pl.ds(pl.multiple_of(exchange_of(near, far, b, False) * blk, blk), blk)
        row = b * blk + lax.broadcasted_iota(jnp.int32, wide, 0)
        keep = jnp.where(row < count[0], jnp.float32(1), jnp.float32(0)).astype(BF)
        mask[at, :] = keep
        both = [xv[m, b * blk : (b + 1) * blk] for m in range(2)]
        h[at, :] = jnp.concatenate(both, axis=1) * keep
    for copy in copies[:2] + copies[3:]:
        copy.wait()
    for k in range(av.shape[0]):
        c = sk[k]
        halo = jnp.where(odd, c, 2 * last + 1 - c)
        at = (
            exchange_of(near, far, sr[k], False),
            jnp.where(c < last, exchange_of(near, far, c, False), halo),
        )
        acc[at] = acc[at] + av[k].astype(F32)
    for r in range(last):
        for c in range(last + 2):
            dense[r * blk : (r + 1) * blk, c * blk : (c + 1) * blk] = acc[r, c].astype(BF)
    at = pl.ds(pl.multiple_of(jnp.where(near == far, 0, 1) * blk, blk), blk)
    df[...] = dense[at, :]


def message_weight(pack, i):
    d = pack.shape[1]
    return twice(pack[i * d : (i + 1) * d])


def first_body(h, pick, haloq, halor, pack, m, halo, nseen):
    w = message_weight(pack, 0)
    m[...] = silu_of_twice(dot(h[...], w))
    blk = nseen.shape[0]
    both = jnp.concatenate([choose(pick, haloq[0, :blk], haloq[1, :blk]), halor[:blk]], axis=0)
    halo[...] = silu_of_twice(dot(both, w))
    nseen[...] = choose(pick, haloq[0, blk:], haloq[1, blk:])


def layer(h, m, halo, dense, mask, pack, i, agg, hidden, c, extra=None):
    d = pack.shape[1]
    n = m.shape[0]
    own = [slice(r, r + CHUNK) for r in range(0, n, CHUNK)]
    chunks = list(own)
    if extra:
        chunks[-1] = slice(n - CHUNK, agg.shape[0])

    def rows(ref, at, j):
        if at.stop <= n:
            return ref[at]
        return jnp.concatenate([ref[at.start : n], extra[j][...]], axis=0)

    wh = pack[2 * d + i * 2 * d : 2 * d + (i + 1) * 2 * d]
    wo = twice(pack[6 * d + i * d : 6 * d + (i + 1) * d])
    v = pack[8 * d :].astype(F32)

    def row(j):
        r = v[j + i : j + i + 1]
        return jnp.concatenate([r, r], axis=1)

    if LOCAL_FIRST:
        for at in own:
            c[at] = dot(dense[at, :n], m[...])
        halo = halo()
        for at in own:
            agg[at] = (c[at] + dot(dense[at, n:], halo)).astype(BF)
    else:
        halo = halo()
        for at in own:
            agg[at] = (dot(dense[at, :n], m[...]) + dot(dense[at, n:], halo)).astype(BF)
    if extra:
        agg[n:] = extra[2]().astype(BF)
    b = row(0)
    for at in chunks:
        now = rows(h, at, 0)
        pre = [
            dot(jnp.concatenate([now[:, s : s + d], agg[at, s : s + d]], axis=1), wh)
            for s in (0, d)
        ]
        hidden[at] = silu_of_twice(jnp.concatenate(pre, axis=1) + b)
    b = row(2) + row(4)
    for at in chunks:
        c[at] = dot(hidden[at], wo) + b
    mean = twice(jnp.full((d, d), 1.0 / d, BF))
    gain = row(6)
    for at in chunks:
        now = c[at]
        var = dot((now * now).astype(BF), mean)
        new = (rows(h, at, 0).astype(F32) + now * lax.rsqrt(var + 1e-05) * gain).astype(BF)
        yield at, new * rows(mask, at, 1)


def send_messages(new_h, new_m, nxt, i):
    w = message_weight(nxt, i)
    for r in range(0, new_m.shape[0], CHUNK):
        at = slice(r, r + CHUNK)
        new_m[at] = silu_of_twice(dot(new_h[at], w))


def far_block(fsel, ref, blk):
    return choose(fsel, ref[:blk], ref[blk : 2 * blk])


def start_body(step):
    def body(h, m, halo, dense, df, mask, fsel, pack, nxt, new_h, new_m, outq, far_h, part, *rest):
        blk = outq.shape[0]
        for at, new in layer(h, m, lambda: halo[...], dense, mask, pack, step % 2, *rest):
            new_h[at] = new
        send_messages(new_h, new_m, nxt, (step + 1) % 2)
        outq[...] = new_m[:blk]
        far_h[...] = far_block(fsel, new_h, blk)
        part[...] = dot(df[:, : new_m.shape[0]], new_m[...])

    return body


def pay_body(pick, haloq, df, far_h, part, pay, near_m):
    blk = far_h.shape[0]
    n = df.shape[1] - 2 * blk
    near = choose(pick, haloq[0], haloq[1])
    near_m[...] = near
    pay[:blk] = far_h[...]
    pay[blk:] = (part[...] + dot(df[:, n : n + blk], near)).astype(BF)


def partner_layer(h, m, given, pick, seen, mine, other, is_far, dense, mask, pack, i, new_h, rest):
    agg, hidden, c, hx, mx = rest
    n = m.shape[0]
    blk, d2 = hx.shape
    d = d2 // 2
    hx[...] = choose(pick, given[0, :blk], given[1, :blk])
    mx[...] = jnp.concatenate([seen[:, d:], seen[:, d:]], axis=1)

    def halo():
        theirs = silu_of_twice(dot(hx[...], message_weight(pack, i)))
        return jnp.concatenate([other, theirs] if is_far else [theirs, other], axis=0)

    def part():
        given_part = choose(pick, given[0, blk:], given[1, blk:]).astype(F32)
        return given_part + dot(seen[:, :d], mine)

    extra = (hx, mx, part)
    for at, new in layer(h, m, halo, dense, mask, pack, i, agg, hidden, c, extra):
        new_h[at.start : min(at.stop, n)] = new[: n - at.start]
        if at.stop > n:
            hx[...] = new[n - at.start :]


def far_layer_body(step):
    def body(h, m, near_m, fpick, far, dense, mask, fsel, seen, pack, nxt, *rest):
        new_h, new_m, pay, far_m = rest[:4]
        rest = rest[4:]
        n, blk = m.shape[0], far_m.shape[0]
        mine = far_block(fsel, m, blk)
        partner_layer(
            h, m, far, fpick, seen[blk:], mine, near_m[...], True, dense, mask, pack, step % 2,
            new_h, rest,
        )
        send_messages(new_h, new_m, nxt, (step + 1) % 2)
        theirs = silu_of_twice(dot(rest[3][...], message_weight(nxt, (step + 1) % 2)))
        far_m[...] = theirs
        pay[:blk] = new_h[:blk]
        part = dot(dense[:blk, :n], new_m[...]) + dot(dense[:blk, n + blk :], theirs)
        pay[blk:] = part.astype(BF)

    return body


def near_layer_body(step, tail):
    def body(h, m, far_m, pick, near, dense, df, mask, fsel, nseen, pack, nxt, *rest):
        new_h, new_m, pay, near_m = rest[:4]
        rest = rest[4:]
        n, blk = m.shape[0], near_m.shape[0]
        partner_layer(
            h, m, near, pick, nseen[...], m[:blk], far_m[...], False, dense, mask, pack, step % 2,
            new_h, rest,
        )
        send_messages(new_h, new_m, nxt, (step + 1) % 2)
        theirs = silu_of_twice(dot(rest[3][...], message_weight(nxt, (step + 1) % 2)))
        near_m[...] = theirs
        if tail:
            pay[...] = far_block(fsel, new_m, blk)
        else:
            pay[:blk] = far_block(fsel, new_h, blk)
            part = dot(df[:, :n], new_m[...]) + dot(df[:, n : n + blk], theirs)
            pay[blk:] = part.astype(BF)

    return body


def last_body(step):
    def body(h, m, near_m, fpick, far, dense, mask, pack, up, down, out, *rest):
        agg, hidden, c, stage, sem = rest
        d = pack.shape[1]
        blk = near_m.shape[0]

        def halo():
            return jnp.concatenate([near_m[...], choose(fpick, far[0], far[1])], axis=0)

        ends = to_partners(up[0], down[0])
        copies = []
        for at, new in layer(h, m, halo, dense, mask, pack, step % 2, agg, hidden, c):
            stage[0, at] = new[:, :d]
            stage[1, at] = new[:, d:]
            for b in range(at.start // blk, at.stop // blk):
                to = pl.multiple_of(exchange_of(*ends, b, True) * blk, blk)
                copies.append(
                    pltpu.make_async_copy(
                        stage.at[:, b * blk : (b + 1) * blk, :],
                        out.at[:, pl.ds(to, blk), :],
                        sem.at[b],
                    )
                )
                copies[-1].start()
        for copy in copies:
            copy.wait()

    return body


def shards(
    features,
    counts,
    row_blocks,
    col_blocks,
    adjacency,
    send_up,
    send_down,
    w_message,
    w_hidden,
    b_hidden,
    w_out,
    b_out,
    gain,
):
    n, d = features.shape[1:]
    blk = adjacency.shape[1]
    doms = lax.axis_size("dom")
    sections = lax.axis_size("section")
    layers = w_message.shape[0]
    steps = layers * sections
    near_pairs = [[i, i + 1] for i in range(0, doms, 2)]
    far_pairs = [[i, i + 1] for i in range(1, doms - 1, 2)]
    across = [(a, b) for a, b in far_pairs] + [(b, a) for a, b in far_pairs]
    far_pairs = far_pairs + [[0, doms - 1]]

    def s(*shape, dtype=BF):
        return jax.ShapeDtypeStruct(shape, dtype)

    def near_gather(q):
        return lax.all_gather(q, "dom", axis_index_groups=near_pairs)

    def fetch(own, k):
        return lax.ppermute(own, "section", [(i, i + k) for i in range(sections - k)])

    def integers(*sizes):
        return [pltpu.SMEM((k,), jnp.int32) for k in sizes]

    def far_gather(q, step):
        groups = []
        for section in range(sections):
            begun = layers * (sections - 1 - section) <= step + 1
            groups += [
                [section * doms + i for i in pair] for pair in (far_pairs if begun else near_pairs)
            ]
        return lax.all_gather(q, ("section", "dom"), axis_index_groups=groups)

    wide = s(blk, 2 * d)
    both = s(2 * blk, 2 * d)
    rows = s(n, 2 * d)
    two = s(2, blk, 2 * d)
    span = n + 2 * blk
    count_k = adjacency.shape[0]
    vec = pltpu.VMEM((layers, d), BF)
    weights = in_hbm(w_message, w_hidden, b_hidden, w_out, b_out, gain)
    own = call(
        pack_body,
        s(layers * 4 * d + 16, d),
        [HB] * 6,
        [
            pltpu.VMEM((layers, d, d), BF),
            pltpu.VMEM((layers, 2 * d, d), BF),
            pltpu.VMEM((layers, d, d), BF),
            vec,
            vec,
            vec,
            pltpu.SemaphoreType.DMA((6,)),
        ],
    )(*weights)
    packs = [fetch(own, sections - 1)]
    graph = [counts, send_up, send_down, *in_hbm(row_blocks, col_blocks, features, adjacency)]
    q, pay = call(
        blocks_body,
        (both, both),
        [SM] * 3 + [HB] * 4,
        integers(count_k, count_k)
        + [
            pltpu.VMEM((2, 2, blk, d), BF),
            pltpu.VMEM(adjacency.shape, BF),
            pltpu.SemaphoreType.DMA((5,)),
        ],
    )(*graph)
    seen = lax.ppermute(pay, "dom", across)
    prep = call(
        prep_body,
        (rows, s(n, span), s(blk, span), rows, two, two, two),
        [SM] * 3 + [HB] * 4,
        integers(count_k, count_k)
        + [
            pltpu.VMEM(features.shape, BF),
            pltpu.VMEM(adjacency.shape, BF),
            pltpu.VMEM((n // blk, n // blk + 2, blk, blk), F32),
            pltpu.SemaphoreType.DMA((4,)),
        ],
        16,
    )
    h, dense, df, mask, pick, fpick, fsel = prep(*graph)
    q, pick = lax.optimization_barrier((q, pick))
    haloq = near_gather(q)
    later, haloq = lax.optimization_barrier((own, haloq))
    packs += [fetch(later, k) for k in range(sections - 2, 0, -1)] + [own]
    m, halo, nseen = call(first_body, (rows, both, wide), [VM] * 5)(h, pick, haloq, seen, packs[0])

    def stages(k):
        return [
            pltpu.VMEM((k, 2 * d), BF),
            pltpu.VMEM((k, 2 * d), BF),
            pltpu.VMEM((k, 2 * d), F32),
        ]

    def weights_at(step):
        return packs[step // layers], packs[(step + 1) // layers]

    h, m, q, far_h, part = call(
        start_body(0), (rows, rows, wide, wide, s(blk, 2 * d, dtype=F32)), [VM] * 9, stages(n)
    )(h, m, halo, dense, df, mask, fsel, *weights_at(0))
    pay, near_m = call(pay_body, (both, wide), [VM] * 5)(pick, near_gather(q), df, far_h, part)
    more = stages(n + blk) + [pltpu.VMEM((blk, 2 * d), BF)] * 2
    for step in range(1, steps - 1, 2):
        asked = far_gather(pay, step)
        h, m, pay, far_m = call(
            far_layer_body(step), (rows, rows, both, wide), [VM] * 11, more
        )(h, m, near_m, fpick, asked, dense, mask, fsel, seen, *weights_at(step))
        asked = near_gather(pay)
        step += 1
        tail = step + 2 == steps
        h, m, pay, near_m = call(
            near_layer_body(step, tail), (rows, rows, wide if tail else both, wide), [VM] * 12, more
        )(h, m, far_m, pick, asked, dense, df, mask, fsel, nseen, *weights_at(step))
    out = call(
        last_body(steps - 1),
        s(2, n, d),
        [VM] * 8 + [SM] * 2,
        stages(n)
        + [pltpu.VMEM((2, n, d), BF)]
        + [pltpu.SemaphoreType.DMA((n // blk,))],
        spaces=HB,
    )(h, m, near_m, fpick, far_gather(pay, steps - 1), dense, mask, packs[-1], send_up, send_down)
    return out[None]


def solution(mesh):
    placed = (
        P(None, "dom", None),
        P("dom"),
        P("dom"),
        P("dom"),
        P("dom", None, None),
        P("dom"),
        P("dom"),
        P("section", None, None),
        P("section", None, None),
        P("section", None),
        P("section", None, None),
        P("section", None),
        P("section", None),
    )
    return jax.shard_map(
        shards,
        mesh=mesh,
        in_specs=placed,
        out_specs=P("section", None, "dom", None),
        check_vma=False,
    )
```

```python
import jax
import jax.numpy as jnp
from jax import lax
from jax.experimental import pallas as pl
from jax.experimental.pallas import tpu as pltpu
from jax.sharding import PartitionSpec as P

BF = jnp.bfloat16
F32 = jnp.float32
VM = pl.BlockSpec(memory_space=pltpu.VMEM)
SM = pl.BlockSpec(memory_space=pltpu.SMEM)
HB = pl.BlockSpec(memory_space=pltpu.HBM)
CHUNK = 512


def call(body, outs, ins, name, scratch=(), room=8, spaces=None):
    return pl.pallas_call(
        body,
        out_shape=outs,
        in_specs=ins,
        out_specs=spaces or jax.tree.map(lambda _: VM, outs),
        scratch_shapes=list(scratch),
        name=name,
        compiler_params=pltpu.CompilerParams(vmem_limit_bytes=room << 20),
    )


def in_hbm(*arrays):
    return [pltpu.with_memory_space_constraint(a, pltpu.HBM) for a in arrays]


def dot(a, b):
    return jnp.dot(a, b, preferred_element_type=F32)


def silu_of_twice(u):
    return (u + u * jnp.tanh(u)).astype(BF)


def twice(w):
    zero = jnp.zeros_like(w)
    return jnp.concatenate(
        [jnp.concatenate([w, zero], axis=1), jnp.concatenate([zero, w], axis=1)], axis=0
    )


def flags(cond, shape):
    return jnp.full(shape, jnp.where(cond, jnp.float32(1), jnp.float32(0)), F32).astype(BF)


def choose(pick, a, b):
    return a * pick[0] + b * pick[1]


def fetch_all(pairs, sem):
    copies = [pltpu.make_async_copy(src, dst, sem.at[i]) for i, (src, dst) in enumerate(pairs)]
    for copy in copies:
        copy.start()
    return copies


def parity():
    return lax.axis_index("dom") % 2


def to_partners(up, down):
    odd = parity() == 1
    return jnp.where(odd, down, up), jnp.where(odd, up, down)


def exchange_of(near, far, block, back):
    moved = jnp.where(far == near, 0, jnp.where(far == 0, near, far))

    def first(b):
        return jnp.where(b == near, 0, jnp.where(b == 0, near, b))

    def second(b):
        swapped = jnp.where(b == moved, 1, jnp.where(b == 1, moved, b))
        return jnp.where(moved == 0, b, swapped)

    return first(second(block)) if back else second(first(block))


def pack_body(wm, wh, bh, wo, bo, gain, out, am, ah, ao, vb, vo, vg, sem):
    d = wm.shape[2]
    for copy in fetch_all([(wm, am), (wh, ah), (wo, ao), (bh, vb), (bo, vo), (gain, vg)], sem):
        copy.wait()
    for i in range(2):
        out[i * d : (i + 1) * d] = (am[i].astype(F32) * 0.5).astype(BF)
        at = 2 * d + i * 2 * d
        out[at : at + 2 * d] = (ah[i].astype(F32) * 0.5).astype(BF)
        w = ao[i].astype(F32)
        at = 6 * d + i * d
        out[at : at + d] = (w - jnp.mean(w, axis=1, keepdims=True)).astype(BF)
    b = vo[...].astype(F32)
    b = b - jnp.mean(b, axis=1, keepdims=True)
    high = b.astype(BF).astype(F32)
    pad = jnp.zeros((8, d), F32)
    vectors = [vb[...].astype(F32) * 0.5, high, b - high, vg[...].astype(F32), pad]
    out[8 * d :] = jnp.concatenate(vectors, axis=0).astype(BF)


def prep_body(
    count, up, down, rows, cols, x, adj,
    h, dense, df, mask, pick, fpick, fsel, q, view,
    sr, sk, xv, av, acc, sem,
):
    n, d = xv.shape[1], xv.shape[2]
    blk = av.shape[1]
    last = n // blk
    copies = fetch_all([(rows, sr), (cols, sk), (x, xv), (adj, av)], sem)
    acc[...] = jnp.zeros_like(acc)
    wide = (blk, 2 * d)
    dom = lax.axis_index("dom")
    odd = parity() == 1
    alone = (dom == 0) | (dom == lax.axis_size("dom") - 1)
    pick[0] = flags(odd, wide)
    pick[1] = flags(jnp.logical_not(odd), wide)
    fpick[0] = flags(jnp.logical_not(odd | alone), wide)
    fpick[1] = flags(odd & jnp.logical_not(alone), wide)
    near, far = to_partners(up[0], down[0])
    fsel[0] = flags(near == far, wide)
    fsel[1] = flags(near != far, wide)
    copies[2].wait()
    for b in range(last):
        at = pl.ds(pl.multiple_of(exchange_of(near, far, b, False) * blk, blk), blk)
        row = b * blk + lax.broadcasted_iota(jnp.int32, wide, 0)
        keep = jnp.where(row < count[0], jnp.float32(1), jnp.float32(0)).astype(BF)
        mask[at, :] = keep
        both = [xv[m, b * blk : (b + 1) * blk] for m in range(2)]
        h[at, :] = jnp.concatenate(both, axis=1) * keep
    for copy in copies[:2] + copies[3:]:
        copy.wait()
    for k in range(av.shape[0]):
        c = sk[k]
        halo = jnp.where(odd, c, 2 * last + 1 - c)
        at = (
            exchange_of(near, far, sr[k], False),
            jnp.where(c < last, exchange_of(near, far, c, False), halo),
        )
        acc[at] = acc[at] + av[k].astype(F32)
    for r in range(last):
        for c in range(last + 2):
            dense[r * blk : (r + 1) * blk, c * blk : (c + 1) * blk] = acc[r, c].astype(BF)
    at = pl.ds(pl.multiple_of(jnp.where(near == far, 0, 1) * blk, blk), blk)
    df[...] = dense[at, :]
    q[:blk] = h[:blk]
    q[blk:] = jnp.concatenate([dense[:blk, n : n + blk], mask[:blk, :d]], axis=1)
    view[...] = jnp.concatenate([df[:, n + blk :], mask[at, :d]], axis=1)


def message_weight(pack, i):
    d = pack.shape[1]
    return twice(pack[i * d : (i + 1) * d])


def first_body(h, pick, fsel, near, df, view, pack, m, near_m, nseen, pay):
    w = message_weight(pack, 0)
    blk = nseen.shape[0]
    n = m.shape[0]
    theirs = silu_of_twice(dot(choose(pick, near[0, :blk], near[1, :blk]), w))
    m[...] = silu_of_twice(dot(h[...], w))
    near_m[...] = theirs
    nseen[...] = choose(pick, near[0, blk:], near[1, blk:])
    pay[:blk] = far_block(fsel, h, blk)
    part = dot(df[:, :n], m[...]) + dot(df[:, n : n + blk], theirs)
    pay[blk : 2 * blk] = part.astype(BF)
    pay[2 * blk :] = view[...]


def layer(h, m, halo, dense, mask, pack, i, agg, hidden, c, extra=None):
    d = pack.shape[1]
    n = m.shape[0]
    own = [slice(r, r + CHUNK) for r in range(0, n, CHUNK)]
    chunks = list(own)
    if extra:
        chunks[-1] = slice(n - CHUNK, agg.shape[0])

    def rows(ref, at, j):
        if at.stop <= n:
            return ref[at]
        return jnp.concatenate([ref[at.start : n], extra[j][...]], axis=0)

    wh = pack[2 * d + i * 2 * d : 2 * d + (i + 1) * 2 * d]
    wo = twice(pack[6 * d + i * d : 6 * d + (i + 1) * d])
    v = pack[8 * d :].astype(F32)

    def row(j):
        r = v[j + i : j + i + 1]
        return jnp.concatenate([r, r], axis=1)

    for at in own:
        c[at] = dot(dense[at, :n], m[...])
    halo = halo()
    for at in own:
        agg[at] = (c[at] + dot(dense[at, n:], halo)).astype(BF)
    if extra:
        agg[n:] = extra[2]().astype(BF)
    b = row(0)
    for at in chunks:
        now = rows(h, at, 0)
        pre = [
            dot(jnp.concatenate([now[:, s : s + d], agg[at, s : s + d]], axis=1), wh)
            for s in (0, d)
        ]
        hidden[at] = silu_of_twice(jnp.concatenate(pre, axis=1) + b)
    b = row(2) + row(4)
    for at in chunks:
        c[at] = dot(hidden[at], wo) + b
    mean = twice(jnp.full((d, d), 1.0 / d, BF))
    gain = row(6)
    for at in chunks:
        now = c[at]
        var = dot((now * now).astype(BF), mean)
        new = (rows(h, at, 0).astype(F32) + now * lax.rsqrt(var + 1e-05) * gain).astype(BF)
        yield at, new * rows(mask, at, 1)


def send_messages(new_h, new_m, nxt, i):
    w = message_weight(nxt, i)
    for r in range(0, new_m.shape[0], CHUNK):
        at = slice(r, r + CHUNK)
        new_m[at] = silu_of_twice(dot(new_h[at], w))


def far_block(fsel, ref, blk):
    return choose(fsel, ref[:blk], ref[blk : 2 * blk])


def partner_layer(h, m, given, pick, seen, mine, other, is_far, dense, mask, pack, i, new_h, rest):
    agg, hidden, c, hx, mx = rest
    n = m.shape[0]
    blk, d2 = hx.shape
    d = d2 // 2
    hx[...] = choose(pick, given[0, :blk], given[1, :blk])
    mx[...] = jnp.concatenate([seen[:, d:], seen[:, d:]], axis=1)

    def halo():
        theirs = silu_of_twice(dot(hx[...], message_weight(pack, i)))
        return jnp.concatenate([other, theirs] if is_far else [theirs, other], axis=0)

    def part():
        given_part = choose(pick, given[0, blk : 2 * blk], given[1, blk : 2 * blk]).astype(F32)
        return given_part + dot(seen[:, :d], mine)

    extra = (hx, mx, part)
    for at, new in layer(h, m, halo, dense, mask, pack, i, agg, hidden, c, extra):
        new_h[at.start : min(at.stop, n)] = new[: n - at.start]
        if at.stop > n:
            hx[...] = new[n - at.start :]


def far_layer_body(step, begin, tail):
    def body(h, m, near_m, fpick, far, dense, mask, fsel, seen, pack, nxt, *rest):
        new_h, new_m, pay, far_m = rest[:4]
        n, blk = m.shape[0], far_m.shape[0]
        if begin:
            seen = rest[4]
            seen[...] = choose(fpick, far[0, 2 * blk :], far[1, 2 * blk :])
        rest = rest[-5:]
        mine = far_block(fsel, m, blk)
        partner_layer(
            h, m, far, fpick, seen[...], mine, near_m[...], True, dense, mask, pack, step % 2,
            new_h, rest,
        )
        send_messages(new_h, new_m, nxt, (step + 1) % 2)
        theirs = silu_of_twice(dot(rest[3][...], message_weight(nxt, (step + 1) % 2)))
        far_m[...] = theirs
        if tail:
            pay[...] = new_m[:blk]
        else:
            pay[:blk] = new_h[:blk]
            part = dot(dense[:blk, :n], new_m[...]) + dot(dense[:blk, n + blk :], theirs)
            pay[blk:] = part.astype(BF)

    return body


def near_layer_body(step):
    def body(h, m, far_m, pick, near, dense, df, mask, fsel, nseen, pack, nxt, *rest):
        new_h, new_m, pay, near_m = rest[:4]
        rest = rest[4:]
        n, blk = m.shape[0], near_m.shape[0]
        partner_layer(
            h, m, near, pick, nseen[...], m[:blk], far_m[...], False, dense, mask, pack, step % 2,
            new_h, rest,
        )
        send_messages(new_h, new_m, nxt, (step + 1) % 2)
        theirs = silu_of_twice(dot(rest[3][...], message_weight(nxt, (step + 1) % 2)))
        near_m[...] = theirs
        pay[:blk] = far_block(fsel, new_h, blk)
        part = dot(df[:, :n], new_m[...]) + dot(df[:, n : n + blk], theirs)
        pay[blk:] = part.astype(BF)

    return body


def last_body(step):
    def body(h, m, pick, near, far_m, dense, mask, pack, up, down, out, *rest):
        agg, hidden, c, stage, sem = rest
        d = pack.shape[1]
        blk = far_m.shape[0]

        def halo():
            return jnp.concatenate([choose(pick, near[0], near[1]), far_m[...]], axis=0)

        ends = to_partners(up[0], down[0])
        copies = []
        for at, new in layer(h, m, halo, dense, mask, pack, step % 2, agg, hidden, c):
            stage[0, at] = new[:, :d]
            stage[1, at] = new[:, d:]
            for b in range(at.start // blk, at.stop // blk):
                to = pl.multiple_of(exchange_of(*ends, b, True) * blk, blk)
                copies.append(
                    pltpu.make_async_copy(
                        stage.at[:, b * blk : (b + 1) * blk, :],
                        out.at[:, pl.ds(to, blk), :],
                        sem.at[b],
                    )
                )
                copies[-1].start()
        for copy in copies:
            copy.wait()

    return body


def shards(
    features,
    counts,
    row_blocks,
    col_blocks,
    adjacency,
    send_up,
    send_down,
    w_message,
    w_hidden,
    b_hidden,
    w_out,
    b_out,
    gain,
):
    n, d = features.shape[1:]
    blk = adjacency.shape[1]
    doms = lax.axis_size("dom")
    sections = lax.axis_size("section")
    layers = w_message.shape[0]
    steps = layers * sections
    near_pairs = [[i, i + 1] for i in range(0, doms, 2)]
    far_pairs = [[i, i + 1] for i in range(1, doms - 1, 2)]
    far_pairs = far_pairs + [[0, doms - 1]]

    def s(*shape, dtype=BF):
        return jax.ShapeDtypeStruct(shape, dtype)

    def near_gather(q):
        return lax.all_gather(q, "dom", axis_index_groups=near_pairs)

    def fetch(own, k):
        return lax.ppermute(own, "section", [(i, i + k) for i in range(sections - k)])

    def integers(*sizes):
        return [pltpu.SMEM((k,), jnp.int32) for k in sizes]

    def far_gather(q, step):
        groups = []
        for section in range(sections):
            begun = step == 0 or layers * (sections - 1 - section) <= step + 1
            groups += [
                [section * doms + i for i in pair] for pair in (far_pairs if begun else near_pairs)
            ]
        return lax.all_gather(q, ("section", "dom"), axis_index_groups=groups)

    wide = s(blk, 2 * d)
    both = s(2 * blk, 2 * d)
    rows = s(n, 2 * d)
    two = s(2, blk, 2 * d)
    span = n + 2 * blk
    count_k = adjacency.shape[0]
    vec = pltpu.VMEM((layers, d), BF)
    weights = in_hbm(w_message, w_hidden, b_hidden, w_out, b_out, gain)
    own = call(
        pack_body,
        s(layers * 4 * d + 16, d),
        [HB] * 6,
        "pack",
        [
            pltpu.VMEM((layers, d, d), BF),
            pltpu.VMEM((layers, 2 * d, d), BF),
            pltpu.VMEM((layers, d, d), BF),
            vec,
            vec,
            vec,
            pltpu.SemaphoreType.DMA((6,)),
        ],
    )(*weights)
    packs = [fetch(own, sections - 1)]
    graph = [counts, send_up, send_down, *in_hbm(row_blocks, col_blocks, features, adjacency)]
    h, dense, df, mask, pick, fpick, fsel, q, view = call(
        prep_body,
        (rows, s(n, span), s(blk, span), rows, two, two, two, both, wide),
        [SM] * 3 + [HB] * 4,
        "prep",
        integers(count_k, count_k)
        + [
            pltpu.VMEM(features.shape, BF),
            pltpu.VMEM(adjacency.shape, BF),
            pltpu.VMEM((n // blk, n // blk + 2, blk, blk), F32),
            pltpu.SemaphoreType.DMA((4,)),
        ],
        16,
    )(*graph)
    near = near_gather(q)
    later, near = lax.optimization_barrier((own, near))
    packs += [fetch(later, k) for k in range(sections - 2, 0, -1)] + [own]
    m, near_m, nseen, pay = call(
        first_body, (rows, wide, wide, s(3 * blk, 2 * d)), [VM] * 7, "first"
    )(h, pick, fsel, near, df, view, packs[0])

    def stages(k):
        return [
            pltpu.VMEM((k, 2 * d), BF),
            pltpu.VMEM((k, 2 * d), BF),
            pltpu.VMEM((k, 2 * d), F32),
        ]

    def weights_at(step):
        return packs[step // layers], packs[(step + 1) // layers]

    more = stages(n + blk) + [pltpu.VMEM((blk, 2 * d), BF)] * 2
    seen = view
    for step in range(0, steps, 2):
        tail = step + 2 == steps
        asked = far_gather(pay, step)
        h, m, pay, far_m, *kept = call(
            far_layer_body(step, step == 0, tail),
            (rows, rows, wide if tail else both, wide) + ((wide,) if step == 0 else ()),
            [VM] * 11,
            f"layer{step}",
            more,
        )(h, m, near_m, fpick, asked, dense, mask, fsel, seen, *weights_at(step))
        if kept:
            seen = kept[0]
        asked = near_gather(pay)
        if not tail:
            step += 1
            h, m, pay, near_m = call(
                near_layer_body(step), (rows, rows, both, wide), [VM] * 12, f"layer{step}", more
            )(h, m, far_m, pick, asked, dense, df, mask, fsel, nseen, *weights_at(step))
    out = call(
        last_body(steps - 1),
        s(2, n, d),
        [VM] * 8 + [SM] * 2,
        f"layer{steps - 1}",
        stages(n)
        + [pltpu.VMEM((2, n, d), BF)]
        + [pltpu.SemaphoreType.DMA((n // blk,))],
        spaces=HB,
    )(h, m, pick, asked, far_m, dense, mask, packs[-1], send_up, send_down)
    return out[None]


def solution(mesh):
    placed = (
        P(None, "dom", None),
        P("dom"),
        P("dom"),
        P("dom"),
        P("dom", None, None),
        P("dom"),
        P("dom"),
        P("section", None, None),
        P("section", None, None),
        P("section", None),
        P("section", None, None),
        P("section", None),
        P("section", None),
    )
    return jax.shard_map(
        shards,
        mesh=mesh,
        in_specs=placed,
        out_specs=P("section", None, "dom", None),
        check_vma=False,
    )
```

```python
import jax
import jax.numpy as jnp
from jax import lax
from jax.experimental import pallas as pl
from jax.experimental.pallas import tpu as pltpu
from jax.sharding import PartitionSpec as P

BF = jnp.bfloat16
F32 = jnp.float32
VM = pl.BlockSpec(memory_space=pltpu.VMEM)
SM = pl.BlockSpec(memory_space=pltpu.SMEM)
HB = pl.BlockSpec(memory_space=pltpu.HBM)
CHUNK = 512


def call(body, outs, ins, name, scratch=(), room=8, spaces=None):
    return pl.pallas_call(
        body,
        out_shape=outs,
        in_specs=ins,
        out_specs=spaces or jax.tree.map(lambda _: VM, outs),
        scratch_shapes=list(scratch),
        name=name,
        compiler_params=pltpu.CompilerParams(vmem_limit_bytes=room << 20),
    )


def in_hbm(*arrays):
    return [pltpu.with_memory_space_constraint(a, pltpu.HBM) for a in arrays]


def dot(a, b):
    return jnp.dot(a, b, preferred_element_type=F32)


def silu_of_twice(u):
    return (u + u * jnp.tanh(u)).astype(BF)


def twice(w):
    zero = jnp.zeros_like(w)
    return jnp.concatenate(
        [jnp.concatenate([w, zero], axis=1), jnp.concatenate([zero, w], axis=1)], axis=0
    )


def flags(cond, shape):
    return jnp.full(shape, jnp.where(cond, jnp.float32(1), jnp.float32(0)), F32).astype(BF)


def choose(pick, a, b):
    return a * pick[0] + b * pick[1]


def fetch_all(pairs, sem):
    copies = [pltpu.make_async_copy(src, dst, sem.at[i]) for i, (src, dst) in enumerate(pairs)]
    for copy in copies:
        copy.start()
    return copies


def parity():
    return lax.axis_index("dom") % 2


def to_partners(up, down):
    odd = parity() == 1
    return jnp.where(odd, down, up), jnp.where(odd, up, down)


def exchange_of(near, far, block, back):
    moved = jnp.where(far == near, 0, jnp.where(far == 0, near, far))

    def first(b):
        return jnp.where(b == near, 0, jnp.where(b == 0, near, b))

    def second(b):
        swapped = jnp.where(b == moved, 1, jnp.where(b == 1, moved, b))
        return jnp.where(moved == 0, b, swapped)

    return first(second(block)) if back else second(first(block))


def pack_body(wm, wh, bh, wo, bo, gain, out, am, ah, ao, vb, vo, vg, sem):
    d = wm.shape[2]
    for copy in fetch_all([(wm, am), (wh, ah), (wo, ao), (bh, vb), (bo, vo), (gain, vg)], sem):
        copy.wait()
    for i in range(2):
        out[i * d : (i + 1) * d] = (am[i].astype(F32) * 0.5).astype(BF)
        at = 2 * d + i * 2 * d
        out[at : at + 2 * d] = (ah[i].astype(F32) * 0.5).astype(BF)
        w = ao[i].astype(F32)
        at = 6 * d + i * d
        out[at : at + d] = (w - jnp.mean(w, axis=1, keepdims=True)).astype(BF)
    b = vo[...].astype(F32)
    b = b - jnp.mean(b, axis=1, keepdims=True)
    high = b.astype(BF).astype(F32)
    pad = jnp.zeros((8, d), F32)
    vectors = [vb[...].astype(F32) * 0.5, high, b - high, vg[...].astype(F32), pad]
    out[8 * d :] = jnp.concatenate(vectors, axis=0).astype(BF)


def prep_body(
    count, up, down, rows, cols, x, adj,
    h, dense, df, mask, pick, fpick, fsel, q, view,
    sr, sk, xv, av, acc, sem,
):
    n, d = xv.shape[1], xv.shape[2]
    blk = av.shape[1]
    last = n // blk
    copies = fetch_all([(rows, sr), (cols, sk), (x, xv), (adj, av)], sem)
    acc[...] = jnp.zeros_like(acc)
    wide = (blk, 2 * d)
    dom = lax.axis_index("dom")
    odd = parity() == 1
    alone = (dom == 0) | (dom == lax.axis_size("dom") - 1)
    pick[0] = flags(odd, wide)
    pick[1] = flags(jnp.logical_not(odd), wide)
    fpick[0] = flags(jnp.logical_not(odd | alone), wide)
    fpick[1] = flags(odd & jnp.logical_not(alone), wide)
    near, far = to_partners(up[0], down[0])
    fsel[0] = flags(near == far, wide)
    fsel[1] = flags(near != far, wide)
    copies[2].wait()
    for b in range(last):
        at = pl.ds(pl.multiple_of(exchange_of(near, far, b, False) * blk, blk), blk)
        row = b * blk + lax.broadcasted_iota(jnp.int32, wide, 0)
        keep = jnp.where(row < count[0], jnp.float32(1), jnp.float32(0)).astype(BF)
        mask[at, :] = keep
        both = [xv[m, b * blk : (b + 1) * blk] for m in range(2)]
        h[at, :] = jnp.concatenate(both, axis=1) * keep
    for copy in copies[:2] + copies[3:]:
        copy.wait()
    for k in range(av.shape[0]):
        c = sk[k]
        halo = jnp.where(odd, c, 2 * last + 1 - c)
        at = (
            exchange_of(near, far, sr[k], False),
            jnp.where(c < last, exchange_of(near, far, c, False), halo),
        )
        acc[at] = acc[at] + av[k].astype(F32)
    for r in range(last):
        for c in range(last + 2):
            dense[r * blk : (r + 1) * blk, c * blk : (c + 1) * blk] = acc[r, c].astype(BF)
    at = pl.ds(pl.multiple_of(jnp.where(near == far, 0, 1) * blk, blk), blk)
    df[...] = dense[at, :]
    q[:blk] = h[:blk]
    q[blk:] = jnp.concatenate([dense[:blk, n : n + blk], mask[:blk, :d]], axis=1)
    view[...] = jnp.concatenate([df[:, n + blk :], mask[at, :d]], axis=1)


def message_weight(pack, i):
    d = pack.shape[1]
    return twice(pack[i * d : (i + 1) * d])


def first_body(h, pick, fsel, near, df, view, pack, m, near_m, nseen, pay):
    w = message_weight(pack, 0)
    blk = nseen.shape[0]
    n = m.shape[0]
    theirs = silu_of_twice(dot(choose(pick, near[0, :blk], near[1, :blk]), w))
    m[...] = silu_of_twice(dot(h[...], w))
    near_m[...] = theirs
    nseen[...] = choose(pick, near[0, blk:], near[1, blk:])
    pay[:blk] = far_block(fsel, h, blk)
    part = dot(df[:, :n], m[...]) + dot(df[:, n : n + blk], theirs)
    pay[blk : 2 * blk] = part.astype(BF)
    pay[2 * blk :] = view[...]


def layer(h, m, halo, dense, mask, pack, i, agg, hidden, c, extra=None):
    d = pack.shape[1]
    n = m.shape[0]
    own = [slice(r, r + CHUNK) for r in range(0, n, CHUNK)]
    chunks = list(own)
    if extra:
        chunks[-1] = slice(n - CHUNK, agg.shape[0])

    def rows(ref, at, j):
        if at.stop <= n:
            return ref[at]
        return jnp.concatenate([ref[at.start : n], extra[j][...]], axis=0)

    wh = pack[2 * d + i * 2 * d : 2 * d + (i + 1) * 2 * d]
    wo = twice(pack[6 * d + i * d : 6 * d + (i + 1) * d])
    v = pack[8 * d :].astype(F32)

    def row(j):
        r = v[j + i : j + i + 1]
        return jnp.concatenate([r, r], axis=1)

    for at in own:
        c[at] = dot(dense[at, :n], m[...])
    halo = halo()
    for at in own:
        agg[at] = (c[at] + dot(dense[at, n:], halo)).astype(BF)
    if extra:
        agg[n:] = extra[2]().astype(BF)
    b = row(0)
    for at in chunks:
        now = rows(h, at, 0)
        pre = [
            dot(jnp.concatenate([now[:, s : s + d], agg[at, s : s + d]], axis=1), wh)
            for s in (0, d)
        ]
        hidden[at] = silu_of_twice(jnp.concatenate(pre, axis=1) + b)
    b = row(2) + row(4)
    for at in chunks:
        c[at] = dot(hidden[at], wo) + b
    mean = twice(jnp.full((d, d), 1.0 / d, BF))
    gain = row(6)
    for at in chunks:
        now = c[at]
        var = dot((now * now).astype(BF), mean)
        new = (rows(h, at, 0).astype(F32) + now * lax.rsqrt(var + 1e-05) * gain).astype(BF)
        yield at, new * rows(mask, at, 1)


def send_messages(new_h, new_m, nxt, i):
    w = message_weight(nxt, i)
    for r in range(0, new_m.shape[0], CHUNK):
        at = slice(r, r + CHUNK)
        new_m[at] = silu_of_twice(dot(new_h[at], w))


def far_block(fsel, ref, blk):
    return choose(fsel, ref[:blk], ref[blk : 2 * blk])


def partner_layer(h, m, given, pick, seen, mine, other, is_far, dense, mask, pack, i, new_h, rest):
    agg, hidden, c, hx, mx = rest
    n = m.shape[0]
    blk, d2 = hx.shape
    d = d2 // 2
    hx[...] = choose(pick, given[0, :blk], given[1, :blk])
    mx[...] = jnp.concatenate([seen[:, d:], seen[:, d:]], axis=1)

    def halo():
        theirs = silu_of_twice(dot(hx[...], message_weight(pack, i)))
        return jnp.concatenate([other, theirs] if is_far else [theirs, other], axis=0)

    def part():
        given_part = choose(pick, given[0, blk : 2 * blk], given[1, blk : 2 * blk]).astype(F32)
        return given_part + dot(seen[:, :d], mine)

    extra = (hx, mx, part)
    for at, new in layer(h, m, halo, dense, mask, pack, i, agg, hidden, c, extra):
        new_h[at.start : min(at.stop, n)] = new[: n - at.start]
        if at.stop > n:
            hx[...] = new[n - at.start :]


def far_layer_body(step, begin, tail):
    def body(h, m, near_m, fpick, far, dense, mask, fsel, seen, pack, nxt, *rest):
        new_h, new_m, pay, far_m = rest[:4]
        n, blk = m.shape[0], far_m.shape[0]
        if begin:
            seen = rest[4]
            seen[...] = choose(fpick, far[0, 2 * blk :], far[1, 2 * blk :])
        rest = rest[-5:]
        mine = far_block(fsel, m, blk)
        partner_layer(
            h, m, far, fpick, seen[...], mine, near_m[...], True, dense, mask, pack, step % 2,
            new_h, rest,
        )
        send_messages(new_h, new_m, nxt, (step + 1) % 2)
        theirs = silu_of_twice(dot(rest[3][...], message_weight(nxt, (step + 1) % 2)))
        far_m[...] = theirs
        if tail:
            pay[...] = new_m[:blk]
        else:
            pay[:blk] = new_h[:blk]
            part = dot(dense[:blk, :n], new_m[...]) + dot(dense[:blk, n + blk :], theirs)
            pay[blk:] = part.astype(BF)

    return body


def near_layer_body(step):
    def body(h, m, far_m, pick, near, dense, df, mask, fsel, nseen, pack, nxt, *rest):
        new_h, new_m, pay, near_m = rest[:4]
        rest = rest[4:]
        n, blk = m.shape[0], near_m.shape[0]
        partner_layer(
            h, m, near, pick, nseen[...], m[:blk], far_m[...], False, dense, mask, pack, step % 2,
            new_h, rest,
        )
        send_messages(new_h, new_m, nxt, (step + 1) % 2)
        theirs = silu_of_twice(dot(rest[3][...], message_weight(nxt, (step + 1) % 2)))
        near_m[...] = theirs
        pay[:blk] = far_block(fsel, new_h, blk)
        part = dot(df[:, :n], new_m[...]) + dot(df[:, n : n + blk], theirs)
        pay[blk:] = part.astype(BF)

    return body


def last_body(step):
    def body(h, m, pick, near, far_m, dense, mask, pack, up, down, out, *rest):
        agg, hidden, c, stage, sem = rest
        d = pack.shape[1]
        blk = far_m.shape[0]

        def halo():
            return jnp.concatenate([choose(pick, near[0], near[1]), far_m[...]], axis=0)

        ends = to_partners(up[0], down[0])
        copies = []
        for at, new in layer(h, m, halo, dense, mask, pack, step % 2, agg, hidden, c):
            stage[0, at] = new[:, :d]
            stage[1, at] = new[:, d:]
            for b in range(at.start // blk, at.stop // blk):
                to = pl.multiple_of(exchange_of(*ends, b, True) * blk, blk)
                copies.append(
                    pltpu.make_async_copy(
                        stage.at[:, b * blk : (b + 1) * blk, :],
                        out.at[:, pl.ds(to, blk), :],
                        sem.at[b],
                    )
                )
                copies[-1].start()
        for copy in copies:
            copy.wait()

    return body


def shards(
    features,
    counts,
    row_blocks,
    col_blocks,
    adjacency,
    send_up,
    send_down,
    w_message,
    w_hidden,
    b_hidden,
    w_out,
    b_out,
    gain,
):
    n, d = features.shape[1:]
    blk = adjacency.shape[1]
    doms = lax.axis_size("dom")
    sections = lax.axis_size("section")
    layers = w_message.shape[0]
    steps = layers * sections
    near_pairs = [[i, i + 1] for i in range(0, doms, 2)]
    far_pairs = [[i, i + 1] for i in range(1, doms - 1, 2)]

    def s(*shape, dtype=BF):
        return jax.ShapeDtypeStruct(shape, dtype)

    def near_gather(q):
        return lax.all_gather(q, "dom", axis_index_groups=near_pairs)

    def fetch(own, k):
        return lax.ppermute(own, "section", [(i, i + k) for i in range(sections - k)])

    def integers(*sizes):
        return [pltpu.SMEM((k,), jnp.int32) for k in sizes]

    def far_gather(q, step):
        groups, ends = [], []
        for section in range(sections):
            at = section * doms
            begun = step == 0 or layers * (sections - 1 - section) <= step + 1
            groups += [[at + i for i in pair] for pair in (far_pairs if begun else near_pairs)]
            ends += [at] if begun else []
        if len(ends) % 2:
            groups.append([ends[0], ends[0] + doms - 1])
            ends = ends[1:]
        for a, b in zip(ends[::2], ends[1::2]):
            groups += [[a, b], [a + doms - 1, b + doms - 1]]
        return lax.all_gather(q, ("section", "dom"), axis_index_groups=groups)

    wide = s(blk, 2 * d)
    both = s(2 * blk, 2 * d)
    rows = s(n, 2 * d)
    two = s(2, blk, 2 * d)
    span = n + 2 * blk
    count_k = adjacency.shape[0]
    vec = pltpu.VMEM((layers, d), BF)
    weights = in_hbm(w_message, w_hidden, b_hidden, w_out, b_out, gain)
    own = call(
        pack_body,
        s(layers * 4 * d + 16, d),
        [HB] * 6,
        "pack",
        [
            pltpu.VMEM((layers, d, d), BF),
            pltpu.VMEM((layers, 2 * d, d), BF),
            pltpu.VMEM((layers, d, d), BF),
            vec,
            vec,
            vec,
            pltpu.SemaphoreType.DMA((6,)),
        ],
    )(*weights)
    packs = [fetch(own, sections - 1)]
    graph = [counts, send_up, send_down, *in_hbm(row_blocks, col_blocks, features, adjacency)]
    h, dense, df, mask, pick, fpick, fsel, q, view = call(
        prep_body,
        (rows, s(n, span), s(blk, span), rows, two, two, two, both, wide),
        [SM] * 3 + [HB] * 4,
        "prep",
        integers(count_k, count_k)
        + [
            pltpu.VMEM(features.shape, BF),
            pltpu.VMEM(adjacency.shape, BF),
            pltpu.VMEM((n // blk, n // blk + 2, blk, blk), F32),
            pltpu.SemaphoreType.DMA((4,)),
        ],
        16,
    )(*graph)
    near = near_gather(q)
    later, near = lax.optimization_barrier((own, near))
    packs += [fetch(later, k) for k in range(sections - 2, 0, -1)] + [own]
    m, near_m, nseen, pay = call(
        first_body, (rows, wide, wide, s(3 * blk, 2 * d)), [VM] * 7, "first"
    )(h, pick, fsel, near, df, view, packs[0])

    def stages(k):
        return [
            pltpu.VMEM((k, 2 * d), BF),
            pltpu.VMEM((k, 2 * d), BF),
            pltpu.VMEM((k, 2 * d), F32),
        ]

    def weights_at(step):
        return packs[step // layers], packs[(step + 1) // layers]

    more = stages(n + blk) + [pltpu.VMEM((blk, 2 * d), BF)] * 2
    seen = view
    for step in range(0, steps, 2):
        tail = step + 2 == steps
        asked = far_gather(pay, step)
        h, m, pay, far_m, *kept = call(
            far_layer_body(step, step == 0, tail),
            (rows, rows, wide if tail else both, wide) + ((wide,) if step == 0 else ()),
            [VM] * 11,
            f"layer{step}",
            more,
        )(h, m, near_m, fpick, asked, dense, mask, fsel, seen, *weights_at(step))
        if kept:
            seen = kept[0]
        asked = near_gather(pay)
        if not tail:
            step += 1
            h, m, pay, near_m = call(
                near_layer_body(step), (rows, rows, both, wide), [VM] * 12, f"layer{step}", more
            )(h, m, far_m, pick, asked, dense, df, mask, fsel, nseen, *weights_at(step))
    out = call(
        last_body(steps - 1),
        s(2, n, d),
        [VM] * 8 + [SM] * 2,
        f"layer{steps - 1}",
        stages(n)
        + [pltpu.VMEM((2, n, d), BF)]
        + [pltpu.SemaphoreType.DMA((n // blk,))],
        spaces=HB,
    )(h, m, pick, asked, far_m, dense, mask, packs[-1], send_up, send_down)
    return out[None]


def solution(mesh):
    placed = (
        P(None, "dom", None),
        P("dom"),
        P("dom"),
        P("dom"),
        P("dom", None, None),
        P("dom"),
        P("dom"),
        P("section", None, None),
        P("section", None, None),
        P("section", None),
        P("section", None, None),
        P("section", None),
        P("section", None),
    )
    return jax.shard_map(
        shards,
        mesh=mesh,
        in_specs=placed,
        out_specs=P("section", None, "dom", None),
        check_vma=False,
    )
```

```python
import jax
import jax.numpy as jnp
from jax import lax
from jax.experimental import pallas as pl
from jax.experimental.pallas import tpu as pltpu
from jax.sharding import PartitionSpec as P

BF = jnp.bfloat16
F32 = jnp.float32
VM = pl.BlockSpec(memory_space=pltpu.VMEM)
SM = pl.BlockSpec(memory_space=pltpu.SMEM)
HB = pl.BlockSpec(memory_space=pltpu.HBM)
CHUNK = 512


def call(body, outs, ins, name, scratch=(), room=8, spaces=None):
    return pl.pallas_call(
        body,
        out_shape=outs,
        in_specs=ins,
        out_specs=spaces or jax.tree.map(lambda _: VM, outs),
        scratch_shapes=list(scratch),
        name=name,
        compiler_params=pltpu.CompilerParams(vmem_limit_bytes=room << 20),
    )


def in_hbm(*arrays):
    return [pltpu.with_memory_space_constraint(a, pltpu.HBM) for a in arrays]


def dot(a, b):
    return jnp.dot(a, b, preferred_element_type=F32)


def silu_of_twice(u):
    return (u + u * jnp.tanh(u)).astype(BF)


def twice(w):
    zero = jnp.zeros_like(w)
    return jnp.concatenate(
        [jnp.concatenate([w, zero], axis=1), jnp.concatenate([zero, w], axis=1)], axis=0
    )


def flags(cond, shape):
    return jnp.full(shape, jnp.where(cond, jnp.float32(1), jnp.float32(0)), F32).astype(BF)


def choose(pick, a, b):
    return a * pick[0] + b * pick[1]


def fetch_all(pairs, sem):
    copies = [pltpu.make_async_copy(src, dst, sem.at[i]) for i, (src, dst) in enumerate(pairs)]
    for copy in copies:
        copy.start()
    return copies


def parity():
    return lax.axis_index("dom") % 2


def to_partners(up, down):
    odd = parity() == 1
    return jnp.where(odd, down, up), jnp.where(odd, up, down)


def exchange_of(near, far, block, back):
    moved = jnp.where(far == near, 0, jnp.where(far == 0, near, far))

    def first(b):
        return jnp.where(b == near, 0, jnp.where(b == 0, near, b))

    def second(b):
        swapped = jnp.where(b == moved, 1, jnp.where(b == 1, moved, b))
        return jnp.where(moved == 0, b, swapped)

    return first(second(block)) if back else second(first(block))


def pack_weights(wm, wh, bh, wo, bo, gain, out, am, ah, ao, vb, vo, vg, sem):
    d = wm.shape[2]
    for copy in fetch_all([(wm, am), (wh, ah), (wo, ao), (bh, vb), (bo, vo), (gain, vg)], sem):
        copy.wait()
    for i in range(2):
        out[i * d : (i + 1) * d] = (am[i].astype(F32) * 0.5).astype(BF)
        at = 2 * d + i * 2 * d
        out[at : at + 2 * d] = (ah[i].astype(F32) * 0.5).astype(BF)
        w = ao[i].astype(F32)
        at = 6 * d + i * d
        out[at : at + d] = (w - jnp.mean(w, axis=1, keepdims=True)).astype(BF)
    b = vo[...].astype(F32)
    b = b - jnp.mean(b, axis=1, keepdims=True)
    high = b.astype(BF).astype(F32)
    pad = jnp.zeros((8, d), F32)
    vectors = [vb[...].astype(F32) * 0.5, high, b - high, vg[...].astype(F32), pad]
    out[8 * d :] = jnp.concatenate(vectors, axis=0).astype(BF)


def sends_no_weights():
    return lax.axis_index("section") == lax.axis_size("section") - 1


def pack_body(*refs):
    @pl.when(jnp.logical_not(sends_no_weights()))
    def _():
        pack_weights(*refs)


def pack_late_body(packed, *refs):
    out = refs[6]

    @pl.when(sends_no_weights())
    def _():
        pack_weights(*refs)

    @pl.when(jnp.logical_not(sends_no_weights()))
    def _():
        out[...] = packed[...]


def prep_body(
    count, up, down, rows, cols, x, adj,
    h, dense, df, mask, pick, fpick, fsel, q, view,
    sr, sk, xv, av, acc, sem,
):
    n, d = xv.shape[1], xv.shape[2]
    blk = av.shape[1]
    last = n // blk
    copies = fetch_all([(rows, sr), (cols, sk), (x, xv), (adj, av)], sem)
    acc[...] = jnp.zeros_like(acc)
    wide = (blk, 2 * d)
    dom = lax.axis_index("dom")
    odd = parity() == 1
    alone = (dom == 0) | (dom == lax.axis_size("dom") - 1)
    pick[0] = flags(odd, wide)
    pick[1] = flags(jnp.logical_not(odd), wide)
    fpick[0] = flags(jnp.logical_not(odd | alone), wide)
    fpick[1] = flags(odd & jnp.logical_not(alone), wide)
    near, far = to_partners(up[0], down[0])
    fsel[0] = flags(near == far, wide)
    fsel[1] = flags(near != far, wide)
    copies[2].wait()
    for b in range(last):
        at = pl.ds(pl.multiple_of(exchange_of(near, far, b, False) * blk, blk), blk)
        row = b * blk + lax.broadcasted_iota(jnp.int32, wide, 0)
        keep = jnp.where(row < count[0], jnp.float32(1), jnp.float32(0)).astype(BF)
        mask[at, :] = keep
        both = [xv[m, b * blk : (b + 1) * blk] for m in range(2)]
        h[at, :] = jnp.concatenate(both, axis=1) * keep
    for copy in copies[:2] + copies[3:]:
        copy.wait()
    for k in range(av.shape[0]):
        c = sk[k]
        halo = jnp.where(odd, c, 2 * last + 1 - c)
        at = (
            exchange_of(near, far, sr[k], False),
            jnp.where(c < last, exchange_of(near, far, c, False), halo),
        )
        acc[at] = acc[at] + av[k].astype(F32)
    for r in range(last):
        for c in range(last + 2):
            dense[r * blk : (r + 1) * blk, c * blk : (c + 1) * blk] = acc[r, c].astype(BF)
    at = pl.ds(pl.multiple_of(jnp.where(near == far, 0, 1) * blk, blk), blk)
    df[...] = dense[at, :]
    q[:blk] = h[:blk]
    q[blk:] = jnp.concatenate([dense[:blk, n : n + blk], mask[:blk, :d]], axis=1)
    view[...] = jnp.concatenate([df[:, n + blk :], mask[at, :d]], axis=1)


def message_weight(pack, i):
    d = pack.shape[1]
    return twice(pack[i * d : (i + 1) * d])


def first_body(h, pick, fsel, near, df, view, pack, m, near_m, nseen, pay):
    w = message_weight(pack, 0)
    blk = nseen.shape[0]
    n = m.shape[0]
    theirs = silu_of_twice(dot(choose(pick, near[0, :blk], near[1, :blk]), w))
    m[...] = silu_of_twice(dot(h[...], w))
    near_m[...] = theirs
    nseen[...] = choose(pick, near[0, blk:], near[1, blk:])
    pay[:blk] = far_block(fsel, h, blk)
    part = dot(df[:, :n], m[...]) + dot(df[:, n : n + blk], theirs)
    pay[blk : 2 * blk] = part.astype(BF)
    pay[2 * blk :] = view[...]


def layer(h, m, halo, dense, mask, pack, i, agg, hidden, c, extra=None):
    d = pack.shape[1]
    n = m.shape[0]
    own = [slice(r, r + CHUNK) for r in range(0, n, CHUNK)]
    chunks = list(own)
    if extra:
        chunks[-1] = slice(n - CHUNK, agg.shape[0])

    def rows(ref, at, j):
        if at.stop <= n:
            return ref[at]
        return jnp.concatenate([ref[at.start : n], extra[j][...]], axis=0)

    wh = pack[2 * d + i * 2 * d : 2 * d + (i + 1) * 2 * d]
    wo = twice(pack[6 * d + i * d : 6 * d + (i + 1) * d])
    v = pack[8 * d :].astype(F32)

    def row(j):
        r = v[j + i : j + i + 1]
        return jnp.concatenate([r, r], axis=1)

    for at in own:
        c[at] = dot(dense[at, :n], m[...])
    halo = halo()
    for at in own:
        agg[at] = (c[at] + dot(dense[at, n:], halo)).astype(BF)
    if extra:
        agg[n:] = extra[2]().astype(BF)
    b = row(0)
    for at in chunks:
        now = rows(h, at, 0)
        pre = [
            dot(jnp.concatenate([now[:, s : s + d], agg[at, s : s + d]], axis=1), wh)
            for s in (0, d)
        ]
        hidden[at] = silu_of_twice(jnp.concatenate(pre, axis=1) + b)
    b = row(2) + row(4)
    for at in chunks:
        c[at] = dot(hidden[at], wo) + b
    mean = twice(jnp.full((d, d), 1.0 / d, BF))
    gain = row(6)
    for at in chunks:
        now = c[at]
        var = dot((now * now).astype(BF), mean)
        new = (rows(h, at, 0).astype(F32) + now * lax.rsqrt(var + 1e-05) * gain).astype(BF)
        yield at, new * rows(mask, at, 1)


def send_messages(new_h, new_m, nxt, i):
    w = message_weight(nxt, i)
    for r in range(0, new_m.shape[0], CHUNK):
        at = slice(r, r + CHUNK)
        new_m[at] = silu_of_twice(dot(new_h[at], w))


def far_block(fsel, ref, blk):
    return choose(fsel, ref[:blk], ref[blk : 2 * blk])


def partner_layer(h, m, given, pick, seen, mine, other, is_far, dense, mask, pack, i, new_h, rest):
    agg, hidden, c, hx, mx = rest
    n = m.shape[0]
    blk, d2 = hx.shape
    d = d2 // 2
    hx[...] = choose(pick, given[0, :blk], given[1, :blk])
    mx[...] = jnp.concatenate([seen[:, d:], seen[:, d:]], axis=1)

    def halo():
        theirs = silu_of_twice(dot(hx[...], message_weight(pack, i)))
        return jnp.concatenate([other, theirs] if is_far else [theirs, other], axis=0)

    def part():
        given_part = choose(pick, given[0, blk : 2 * blk], given[1, blk : 2 * blk]).astype(F32)
        return given_part + dot(seen[:, :d], mine)

    extra = (hx, mx, part)
    for at, new in layer(h, m, halo, dense, mask, pack, i, agg, hidden, c, extra):
        new_h[at.start : min(at.stop, n)] = new[: n - at.start]
        if at.stop > n:
            hx[...] = new[n - at.start :]


def far_layer_body(step, begin, tail):
    def body(h, m, near_m, fpick, far, dense, mask, fsel, seen, pack, nxt, *rest):
        new_h, new_m, pay, far_m = rest[:4]
        n, blk = m.shape[0], far_m.shape[0]
        if begin:
            seen = rest[4]
            seen[...] = choose(fpick, far[0, 2 * blk :], far[1, 2 * blk :])
        rest = rest[-5:]
        mine = far_block(fsel, m, blk)
        partner_layer(
            h, m, far, fpick, seen[...], mine, near_m[...], True, dense, mask, pack, step % 2,
            new_h, rest,
        )
        send_messages(new_h, new_m, nxt, (step + 1) % 2)
        theirs = silu_of_twice(dot(rest[3][...], message_weight(nxt, (step + 1) % 2)))
        far_m[...] = theirs
        if tail:
            pay[...] = new_m[:blk]
        else:
            pay[:blk] = new_h[:blk]
            part = dot(dense[:blk, :n], new_m[...]) + dot(dense[:blk, n + blk :], theirs)
            pay[blk:] = part.astype(BF)

    return body


def near_layer_body(step):
    def body(h, m, far_m, pick, near, dense, df, mask, fsel, nseen, pack, nxt, *rest):
        new_h, new_m, pay, near_m = rest[:4]
        rest = rest[4:]
        n, blk = m.shape[0], near_m.shape[0]
        partner_layer(
            h, m, near, pick, nseen[...], m[:blk], far_m[...], False, dense, mask, pack, step % 2,
            new_h, rest,
        )
        send_messages(new_h, new_m, nxt, (step + 1) % 2)
        theirs = silu_of_twice(dot(rest[3][...], message_weight(nxt, (step + 1) % 2)))
        near_m[...] = theirs
        pay[:blk] = far_block(fsel, new_h, blk)
        part = dot(df[:, :n], new_m[...]) + dot(df[:, n : n + blk], theirs)
        pay[blk:] = part.astype(BF)

    return body


def last_body(step):
    def body(h, m, pick, near, far_m, dense, mask, pack, up, down, out, *rest):
        agg, hidden, c, stage, sem = rest
        d = pack.shape[1]
        blk = far_m.shape[0]

        def halo():
            return jnp.concatenate([choose(pick, near[0], near[1]), far_m[...]], axis=0)

        ends = to_partners(up[0], down[0])
        copies = []
        for at, new in layer(h, m, halo, dense, mask, pack, step % 2, agg, hidden, c):
            stage[0, at] = new[:, :d]
            stage[1, at] = new[:, d:]
            for b in range(at.start // blk, at.stop // blk):
                to = pl.multiple_of(exchange_of(*ends, b, True) * blk, blk)
                copies.append(
                    pltpu.make_async_copy(
                        stage.at[:, b * blk : (b + 1) * blk, :],
                        out.at[:, pl.ds(to, blk), :],
                        sem.at[b],
                    )
                )
                copies[-1].start()
        for copy in copies:
            copy.wait()

    return body


def shards(
    features,
    counts,
    row_blocks,
    col_blocks,
    adjacency,
    send_up,
    send_down,
    w_message,
    w_hidden,
    b_hidden,
    w_out,
    b_out,
    gain,
):
    n, d = features.shape[1:]
    blk = adjacency.shape[1]
    doms = lax.axis_size("dom")
    sections = lax.axis_size("section")
    layers = w_message.shape[0]
    steps = layers * sections
    near_pairs = [[i, i + 1] for i in range(0, doms, 2)]
    far_pairs = [[i, i + 1] for i in range(1, doms - 1, 2)]

    def s(*shape, dtype=BF):
        return jax.ShapeDtypeStruct(shape, dtype)

    def near_gather(q):
        return lax.all_gather(q, "dom", axis_index_groups=near_pairs)

    def fetch(own, k):
        return lax.ppermute(own, "section", [(i, i + k) for i in range(sections - k)])

    def integers(*sizes):
        return [pltpu.SMEM((k,), jnp.int32) for k in sizes]

    def far_gather(q, step):
        groups, ends = [], []
        for section in range(sections):
            at = section * doms
            begun = step == 0 or layers * (sections - 1 - section) <= step + 1
            groups += [[at + i for i in pair] for pair in (far_pairs if begun else near_pairs)]
            if begun and (step == 0 or section >= sections - 2):
                ends.append(at)
            elif begun:
                groups.append([at, at + doms - 1])
        for a, b in zip(ends[::2], ends[1::2]):
            groups += [[a, b], [a + doms - 1, b + doms - 1]]
        return lax.all_gather(q, ("section", "dom"), axis_index_groups=groups)

    wide = s(blk, 2 * d)
    both = s(2 * blk, 2 * d)
    rows = s(n, 2 * d)
    two = s(2, blk, 2 * d)
    span = n + 2 * blk
    count_k = adjacency.shape[0]
    vec = pltpu.VMEM((layers, d), BF)
    weights = in_hbm(w_message, w_hidden, b_hidden, w_out, b_out, gain)
    packed = s(layers * 4 * d + 16, d)
    pack_scratch = [
        pltpu.VMEM((layers, d, d), BF),
        pltpu.VMEM((layers, 2 * d, d), BF),
        pltpu.VMEM((layers, d, d), BF),
        vec,
        vec,
        vec,
        pltpu.SemaphoreType.DMA((6,)),
    ]
    own = call(pack_body, packed, [HB] * 6, "pack", pack_scratch)(*weights)
    packs = [fetch(own, sections - 1)]
    graph = [counts, send_up, send_down, *in_hbm(row_blocks, col_blocks, features, adjacency)]
    h, dense, df, mask, pick, fpick, fsel, q, view = call(
        prep_body,
        (rows, s(n, span), s(blk, span), rows, two, two, two, both, wide),
        [SM] * 3 + [HB] * 4,
        "prep",
        integers(count_k, count_k)
        + [
            pltpu.VMEM(features.shape, BF),
            pltpu.VMEM(adjacency.shape, BF),
            pltpu.VMEM((n // blk, n // blk + 2, blk, blk), F32),
            pltpu.SemaphoreType.DMA((4,)),
        ],
        16,
    )(*graph)
    near = near_gather(q)
    later, near = lax.optimization_barrier((own, near))
    packs += [fetch(later, k) for k in range(sections - 2, 0, -1)]
    own = call(pack_late_body, packed, [VM] + [HB] * 6, "pack_late", pack_scratch)(later, *weights)
    own, near = lax.optimization_barrier((own, near))
    packs.append(own)
    m, near_m, nseen, pay = call(
        first_body, (rows, wide, wide, s(3 * blk, 2 * d)), [VM] * 7, "first"
    )(h, pick, fsel, near, df, view, packs[0])

    def stages(k):
        return [
            pltpu.VMEM((k, 2 * d), BF),
            pltpu.VMEM((k, 2 * d), BF),
            pltpu.VMEM((k, 2 * d), F32),
        ]

    def weights_at(step):
        return packs[step // layers], packs[(step + 1) // layers]

    more = stages(n + blk) + [pltpu.VMEM((blk, 2 * d), BF)] * 2
    seen = view
    for step in range(0, steps, 2):
        tail = step + 2 == steps
        asked = far_gather(pay, step)
        h, m, pay, far_m, *kept = call(
            far_layer_body(step, step == 0, tail),
            (rows, rows, wide if tail else both, wide) + ((wide,) if step == 0 else ()),
            [VM] * 11,
            f"layer{step}",
            more,
        )(h, m, near_m, fpick, asked, dense, mask, fsel, seen, *weights_at(step))
        if kept:
            seen = kept[0]
        asked = near_gather(pay)
        if not tail:
            step += 1
            h, m, pay, near_m = call(
                near_layer_body(step), (rows, rows, both, wide), [VM] * 12, f"layer{step}", more
            )(h, m, far_m, pick, asked, dense, df, mask, fsel, nseen, *weights_at(step))
    out = call(
        last_body(steps - 1),
        s(2, n, d),
        [VM] * 8 + [SM] * 2,
        f"layer{steps - 1}",
        stages(n)
        + [pltpu.VMEM((2, n, d), BF)]
        + [pltpu.SemaphoreType.DMA((n // blk,))],
        spaces=HB,
    )(h, m, pick, asked, far_m, dense, mask, packs[-1], send_up, send_down)
    return out[None]


def solution(mesh):
    placed = (
        P(None, "dom", None),
        P("dom"),
        P("dom"),
        P("dom"),
        P("dom", None, None),
        P("dom"),
        P("dom"),
        P("section", None, None),
        P("section", None, None),
        P("section", None),
        P("section", None, None),
        P("section", None),
        P("section", None),
    )
    return jax.shard_map(
        shards,
        mesh=mesh,
        in_specs=placed,
        out_specs=P("section", None, "dom", None),
        check_vma=False,
    )
```

```python
import jax
import jax.numpy as jnp
from jax import lax
from jax.experimental import pallas as pl
from jax.experimental.pallas import tpu as pltpu
from jax.sharding import PartitionSpec as P

BF = jnp.bfloat16
F32 = jnp.float32
VM = pl.BlockSpec(memory_space=pltpu.VMEM)
SM = pl.BlockSpec(memory_space=pltpu.SMEM)
HB = pl.BlockSpec(memory_space=pltpu.HBM)
CHUNK = 512


def call(body, outs, ins, name, scratch=(), room=8, spaces=None):
    return pl.pallas_call(
        body,
        out_shape=outs,
        in_specs=ins,
        out_specs=spaces or jax.tree.map(lambda _: VM, outs),
        scratch_shapes=list(scratch),
        name=name,
        compiler_params=pltpu.CompilerParams(vmem_limit_bytes=room << 20),
    )


def in_hbm(*arrays):
    return [pltpu.with_memory_space_constraint(a, pltpu.HBM) for a in arrays]


def dot(a, b):
    return jnp.dot(a, b, preferred_element_type=F32)


def silu_of_twice(u):
    return (u + u * jnp.tanh(u)).astype(BF)


def twice(w):
    zero = jnp.zeros_like(w)
    return jnp.concatenate(
        [jnp.concatenate([w, zero], axis=1), jnp.concatenate([zero, w], axis=1)], axis=0
    )


def flags(cond, shape):
    return jnp.full(shape, jnp.where(cond, jnp.float32(1), jnp.float32(0)), F32).astype(BF)


def choose(pick, a, b):
    return a * pick[0] + b * pick[1]


def fetch_all(pairs, sem):
    copies = [pltpu.make_async_copy(src, dst, sem.at[i]) for i, (src, dst) in enumerate(pairs)]
    for copy in copies:
        copy.start()
    return copies


def parity():
    return lax.axis_index("dom") % 2


def to_partners(up, down):
    odd = parity() == 1
    return jnp.where(odd, down, up), jnp.where(odd, up, down)


def exchange_of(near, far, block, back):
    moved = jnp.where(far == near, 0, jnp.where(far == 0, near, far))

    def first(b):
        return jnp.where(b == near, 0, jnp.where(b == 0, near, b))

    def second(b):
        swapped = jnp.where(b == moved, 1, jnp.where(b == 1, moved, b))
        return jnp.where(moved == 0, b, swapped)

    return first(second(block)) if back else second(first(block))


def pack_weights(wm, wh, bh, wo, bo, gain, out, am, ah, ao, vb, vo, vg, sem):
    d = wm.shape[2]
    for copy in fetch_all([(wm, am), (wh, ah), (wo, ao), (bh, vb), (bo, vo), (gain, vg)], sem):
        copy.wait()
    for i in range(2):
        out[i * d : (i + 1) * d] = (am[i].astype(F32) * 0.5).astype(BF)
        at = 2 * d + i * 2 * d
        out[at : at + 2 * d] = (ah[i].astype(F32) * 0.5).astype(BF)
        w = ao[i].astype(F32)
        at = 6 * d + i * d
        out[at : at + d] = (w - jnp.mean(w, axis=1, keepdims=True)).astype(BF)
    b = vo[...].astype(F32)
    b = b - jnp.mean(b, axis=1, keepdims=True)
    high = b.astype(BF).astype(F32)
    pad = jnp.zeros((8, d), F32)
    vectors = [vb[...].astype(F32) * 0.5, high, b - high, vg[...].astype(F32), pad]
    out[8 * d :] = jnp.concatenate(vectors, axis=0).astype(BF)


def sends_no_weights():
    return lax.axis_index("section") == lax.axis_size("section") - 1


def pack_body(*refs):
    @pl.when(jnp.logical_not(sends_no_weights()))
    def _():
        pack_weights(*refs)


def pack_late_body(packed, *refs):
    out = refs[6]

    @pl.when(sends_no_weights())
    def _():
        pack_weights(*refs)

    @pl.when(jnp.logical_not(sends_no_weights()))
    def _():
        out[...] = packed[...]


def prep_body(
    count, up, down, rows, cols, x, adj,
    h, dense, df, mask, pick, fpick, fsel, q, view,
    sr, sk, xv, av, acc, sem,
):
    n, d = xv.shape[1], xv.shape[2]
    blk = av.shape[1]
    last = n // blk
    copies = fetch_all([(rows, sr), (cols, sk), (x, xv), (adj, av)], sem)
    acc[...] = jnp.zeros_like(acc)
    wide = (blk, 2 * d)
    dom = lax.axis_index("dom")
    odd = parity() == 1
    alone = (dom == 0) | (dom == lax.axis_size("dom") - 1)
    pick[0] = flags(odd, wide)
    pick[1] = flags(jnp.logical_not(odd), wide)
    fpick[0] = flags(jnp.logical_not(odd | alone), wide)
    fpick[1] = flags(odd & jnp.logical_not(alone), wide)
    near, far = to_partners(up[0], down[0])
    fsel[0] = flags(near == far, wide)
    fsel[1] = flags(near != far, wide)
    copies[2].wait()
    for b in range(last):
        at = pl.ds(pl.multiple_of(exchange_of(near, far, b, False) * blk, blk), blk)
        row = b * blk + lax.broadcasted_iota(jnp.int32, wide, 0)
        keep = jnp.where(row < count[0], jnp.float32(1), jnp.float32(0)).astype(BF)
        mask[at, :] = keep
        both = [xv[m, b * blk : (b + 1) * blk] for m in range(2)]
        h[at, :] = jnp.concatenate(both, axis=1) * keep
    for copy in copies[:2] + copies[3:]:
        copy.wait()
    for k in range(av.shape[0]):
        c = sk[k]
        halo = jnp.where(odd, c, 2 * last + 1 - c)
        at = (
            exchange_of(near, far, sr[k], False),
            jnp.where(c < last, exchange_of(near, far, c, False), halo),
        )
        acc[at] = acc[at] + av[k].astype(F32)
    for r in range(last):
        for c in range(last + 2):
            dense[r * blk : (r + 1) * blk, c * blk : (c + 1) * blk] = acc[r, c].astype(BF)
    at = pl.ds(pl.multiple_of(jnp.where(near == far, 0, 1) * blk, blk), blk)
    df[...] = dense[at, :]
    q[:blk] = h[:blk]
    q[blk:] = jnp.concatenate([dense[:blk, n : n + blk], mask[:blk, :d]], axis=1)
    view[...] = jnp.concatenate([df[:, n + blk :], mask[at, :d]], axis=1)


def message_weight(pack, i):
    d = pack.shape[1]
    return twice(pack[i * d : (i + 1) * d])


def first_body(h, pick, fsel, near, df, view, pack, m, near_m, nseen, pay):
    w = message_weight(pack, 0)
    blk = nseen.shape[0]
    n = m.shape[0]
    theirs = silu_of_twice(dot(choose(pick, near[0, :blk], near[1, :blk]), w))
    m[...] = silu_of_twice(dot(h[...], w))
    near_m[...] = theirs
    nseen[...] = choose(pick, near[0, blk:], near[1, blk:])
    pay[:blk] = far_block(fsel, h, blk)
    part = dot(df[:, :n], m[...]) + dot(df[:, n : n + blk], theirs)
    pay[blk : 2 * blk] = part.astype(BF)
    pay[2 * blk :] = view[...]


def layer(h, m, halo, dense, mask, pack, i, agg, hidden, c, extra=None):
    d = pack.shape[1]
    n = m.shape[0]
    own = [slice(r, r + CHUNK) for r in range(0, n, CHUNK)]
    chunks = list(own)
    if extra:
        chunks[-1] = slice(n - CHUNK, agg.shape[0])

    def rows(ref, at, j):
        if at.stop <= n:
            return ref[at]
        return jnp.concatenate([ref[at.start : n], extra[j][...]], axis=0)

    wh = pack[2 * d + i * 2 * d : 2 * d + (i + 1) * 2 * d]
    wo = twice(pack[6 * d + i * d : 6 * d + (i + 1) * d])
    v = pack[8 * d :].astype(F32)

    def row(j):
        r = v[j + i : j + i + 1]
        return jnp.concatenate([r, r], axis=1)

    for at in own:
        c[at] = dot(dense[at, :n], m[...])
    halo = halo()
    for at in own:
        agg[at] = (c[at] + dot(dense[at, n:], halo)).astype(BF)
    if extra:
        agg[n:] = extra[2]().astype(BF)
    b = row(0)
    for at in chunks:
        now = rows(h, at, 0)
        pre = [
            dot(jnp.concatenate([now[:, s : s + d], agg[at, s : s + d]], axis=1), wh)
            for s in (0, d)
        ]
        hidden[at] = silu_of_twice(jnp.concatenate(pre, axis=1) + b)
    b = row(2) + row(4)
    for at in chunks:
        c[at] = dot(hidden[at], wo) + b
    mean = twice(jnp.full((d, d), 1.0 / d, BF))
    gain = row(6)
    for at in chunks:
        now = c[at]
        var = dot((now * now).astype(BF), mean)
        new = (rows(h, at, 0).astype(F32) + now * lax.rsqrt(var + 1e-05) * gain).astype(BF)
        yield at, new * rows(mask, at, 1)


def send_messages(new_h, new_m, nxt, i):
    w = message_weight(nxt, i)
    for r in range(0, new_m.shape[0], CHUNK):
        at = slice(r, r + CHUNK)
        new_m[at] = silu_of_twice(dot(new_h[at], w))


def far_block(fsel, ref, blk):
    return choose(fsel, ref[:blk], ref[blk : 2 * blk])


def partner_layer(h, m, given, pick, seen, mine, other, is_far, dense, mask, pack, i, new_h, rest):
    agg, hidden, c, hx, mx = rest
    n = m.shape[0]
    blk, d2 = hx.shape
    d = d2 // 2
    hx[...] = choose(pick, given[0, :blk], given[1, :blk])
    mx[...] = jnp.concatenate([seen[:, d:], seen[:, d:]], axis=1)

    def halo():
        theirs = silu_of_twice(dot(hx[...], message_weight(pack, i)))
        return jnp.concatenate([other, theirs] if is_far else [theirs, other], axis=0)

    def part():
        given_part = choose(pick, given[0, blk : 2 * blk], given[1, blk : 2 * blk]).astype(F32)
        return given_part + dot(seen[:, :d], mine)

    extra = (hx, mx, part)
    for at, new in layer(h, m, halo, dense, mask, pack, i, agg, hidden, c, extra):
        new_h[at.start : min(at.stop, n)] = new[: n - at.start]
        if at.stop > n:
            hx[...] = new[n - at.start :]


def far_layer_body(step, begin, tail):
    def body(h, m, near_m, fpick, far, dense, mask, fsel, seen, pack, nxt, *rest):
        new_h, new_m, pay, far_m = rest[:4]
        n, blk = m.shape[0], far_m.shape[0]
        if begin:
            seen = rest[4]
            seen[...] = choose(fpick, far[0, 2 * blk :], far[1, 2 * blk :])
        rest = rest[-5:]
        mine = far_block(fsel, m, blk)
        partner_layer(
            h, m, far, fpick, seen[...], mine, near_m[...], True, dense, mask, pack, step % 2,
            new_h, rest,
        )
        send_messages(new_h, new_m, nxt, (step + 1) % 2)
        theirs = silu_of_twice(dot(rest[3][...], message_weight(nxt, (step + 1) % 2)))
        far_m[...] = theirs
        if tail:
            pay[...] = new_m[:blk]
        else:
            pay[:blk] = new_h[:blk]
            part = dot(dense[:blk, :n], new_m[...]) + dot(dense[:blk, n + blk :], theirs)
            pay[blk:] = part.astype(BF)

    return body


def near_layer_body(step):
    def body(h, m, far_m, pick, near, dense, df, mask, fsel, nseen, pack, nxt, *rest):
        new_h, new_m, pay, near_m = rest[:4]
        rest = rest[4:]
        n, blk = m.shape[0], near_m.shape[0]
        partner_layer(
            h, m, near, pick, nseen[...], m[:blk], far_m[...], False, dense, mask, pack, step % 2,
            new_h, rest,
        )
        send_messages(new_h, new_m, nxt, (step + 1) % 2)
        theirs = silu_of_twice(dot(rest[3][...], message_weight(nxt, (step + 1) % 2)))
        near_m[...] = theirs
        pay[:blk] = far_block(fsel, new_h, blk)
        part = dot(df[:, :n], new_m[...]) + dot(df[:, n : n + blk], theirs)
        pay[blk:] = part.astype(BF)

    return body


def last_body(step):
    def body(h, m, pick, near, far_m, dense, mask, pack, up, down, out, *rest):
        agg, hidden, c, stage, sem = rest
        d = pack.shape[1]
        blk = far_m.shape[0]

        def halo():
            return jnp.concatenate([choose(pick, near[0], near[1]), far_m[...]], axis=0)

        ends = to_partners(up[0], down[0])
        copies = []
        for at, new in layer(h, m, halo, dense, mask, pack, step % 2, agg, hidden, c):
            stage[0, at] = new[:, :d]
            stage[1, at] = new[:, d:]
            for b in range(at.start // blk, at.stop // blk):
                to = pl.multiple_of(exchange_of(*ends, b, True) * blk, blk)
                copies.append(
                    pltpu.make_async_copy(
                        stage.at[:, b * blk : (b + 1) * blk, :],
                        out.at[:, pl.ds(to, blk), :],
                        sem.at[b],
                    )
                )
                copies[-1].start()
        for copy in copies:
            copy.wait()

    return body


def shards(
    features,
    counts,
    row_blocks,
    col_blocks,
    adjacency,
    send_up,
    send_down,
    w_message,
    w_hidden,
    b_hidden,
    w_out,
    b_out,
    gain,
):
    n, d = features.shape[1:]
    blk = adjacency.shape[1]
    doms = lax.axis_size("dom")
    sections = lax.axis_size("section")
    layers = w_message.shape[0]
    steps = layers * sections
    near_pairs = [[i, i + 1] for i in range(0, doms, 2)]
    far_pairs = [[i, i + 1] for i in range(1, doms - 1, 2)]

    def s(*shape, dtype=BF):
        return jax.ShapeDtypeStruct(shape, dtype)

    def near_gather(q):
        return lax.all_gather(q, "dom", axis_index_groups=near_pairs)

    def fetch(own, k):
        return lax.ppermute(own, "section", [(i, i + k) for i in range(sections - k)])

    def integers(*sizes):
        return [pltpu.SMEM((k,), jnp.int32) for k in sizes]

    def far_gather(q, step):
        groups = []
        for section in range(0, sections, 2):
            begun = step == 0 or layers * (sections - 2 - section) <= step + 1
            a, b = section * doms, (section + 1) * doms
            for at in (a, b):
                groups += [[at + i for i in pair] for pair in (far_pairs if begun else near_pairs)]
            if begun:
                groups += [[a, b], [a + doms - 1, b + doms - 1]]
        return lax.all_gather(q, ("section", "dom"), axis_index_groups=groups)

    wide = s(blk, 2 * d)
    both = s(2 * blk, 2 * d)
    rows = s(n, 2 * d)
    two = s(2, blk, 2 * d)
    span = n + 2 * blk
    count_k = adjacency.shape[0]
    vec = pltpu.VMEM((layers, d), BF)
    weights = in_hbm(w_message, w_hidden, b_hidden, w_out, b_out, gain)
    packed = s(layers * 4 * d + 16, d)
    pack_scratch = [
        pltpu.VMEM((layers, d, d), BF),
        pltpu.VMEM((layers, 2 * d, d), BF),
        pltpu.VMEM((layers, d, d), BF),
        vec,
        vec,
        vec,
        pltpu.SemaphoreType.DMA((6,)),
    ]
    own = call(pack_body, packed, [HB] * 6, "pack", pack_scratch)(*weights)
    packs = [fetch(own, sections - 1)]
    graph = [counts, send_up, send_down, *in_hbm(row_blocks, col_blocks, features, adjacency)]
    h, dense, df, mask, pick, fpick, fsel, q, view = call(
        prep_body,
        (rows, s(n, span), s(blk, span), rows, two, two, two, both, wide),
        [SM] * 3 + [HB] * 4,
        "prep",
        integers(count_k, count_k)
        + [
            pltpu.VMEM(features.shape, BF),
            pltpu.VMEM(adjacency.shape, BF),
            pltpu.VMEM((n // blk, n // blk + 2, blk, blk), F32),
            pltpu.SemaphoreType.DMA((4,)),
        ],
        16,
    )(*graph)
    near = near_gather(q)
    later, near = lax.optimization_barrier((own, near))
    packs += [fetch(later, k) for k in range(sections - 2, 0, -1)]
    own = call(pack_late_body, packed, [VM] + [HB] * 6, "pack_late", pack_scratch)(later, *weights)
    own, near = lax.optimization_barrier((own, near))
    packs.append(own)
    m, near_m, nseen, pay = call(
        first_body, (rows, wide, wide, s(3 * blk, 2 * d)), [VM] * 7, "first"
    )(h, pick, fsel, near, df, view, packs[0])

    def stages(k):
        return [
            pltpu.VMEM((k, 2 * d), BF),
            pltpu.VMEM((k, 2 * d), BF),
            pltpu.VMEM((k, 2 * d), F32),
        ]

    def weights_at(step):
        return packs[step // layers], packs[(step + 1) // layers]

    more = stages(n + blk) + [pltpu.VMEM((blk, 2 * d), BF)] * 2
    seen = view
    for step in range(0, steps, 2):
        tail = step + 2 == steps
        asked = far_gather(pay, step)
        h, m, pay, far_m, *kept = call(
            far_layer_body(step, step == 0, tail),
            (rows, rows, wide if tail else both, wide) + ((wide,) if step == 0 else ()),
            [VM] * 11,
            f"layer{step}",
            more,
        )(h, m, near_m, fpick, asked, dense, mask, fsel, seen, *weights_at(step))
        if kept:
            seen = kept[0]
        asked = near_gather(pay)
        if not tail:
            step += 1
            h, m, pay, near_m = call(
                near_layer_body(step), (rows, rows, both, wide), [VM] * 12, f"layer{step}", more
            )(h, m, far_m, pick, asked, dense, df, mask, fsel, nseen, *weights_at(step))
    out = call(
        last_body(steps - 1),
        s(2, n, d),
        [VM] * 8 + [SM] * 2,
        f"layer{steps - 1}",
        stages(n)
        + [pltpu.VMEM((2, n, d), BF)]
        + [pltpu.SemaphoreType.DMA((n // blk,))],
        spaces=HB,
    )(h, m, pick, asked, far_m, dense, mask, packs[-1], send_up, send_down)
    return out[None]


def solution(mesh):
    placed = (
        P(None, "dom", None),
        P("dom"),
        P("dom"),
        P("dom"),
        P("dom", None, None),
        P("dom"),
        P("dom"),
        P("section", None, None),
        P("section", None, None),
        P("section", None),
        P("section", None, None),
        P("section", None),
        P("section", None),
    )
    return jax.shard_map(
        shards,
        mesh=mesh,
        in_specs=placed,
        out_specs=P("section", None, "dom", None),
        check_vma=False,
    )
```
